32 devices in a mesh: groups: 2 (over y), seq: 4 (over z), head: 2 (over x), sub: 2 (over core).
Axes of the slice: x: 2, y: 2, z: 4, core: 2. Of those that a mesh axis runs over, the one named last changes fastest.
Arguments:
- queries: bfloat16 [3072, 8192], P(('groups', 'seq', 'head', 'sub')), parts along dimension 0, may hold values from -128 to 128
- new_keys: bfloat16 [3072, 8192], P(('groups', 'seq', 'head', 'sub')), parts along dimension 0, may hold values from -4 to 4
- new_values: bfloat16 [3072, 8192], P(('groups', 'seq', 'head', 'sub')), parts along dimension 0, may hold values from -6 to 6
- key_cache: bfloat16 [2048, 8192], P(('groups', 'seq'), ('head', 'sub')), parts along dimension 0, may hold values from -6 to 6
- value_cache: bfloat16 [2048, 8192], P(('groups', 'seq'), ('head', 'sub')), parts along dimension 0, may hold values from -6 to 6
- selection: int32 [8, 2], P('groups'), parts along dimension 0, may hold values from 0 to 15, as said below
Outputs:
- attended: bfloat16 [3072, 8192], P(('groups', 'seq', 'head', 'sub')), parts along dimension 0
The draws below stay inside these ranges and needn't reach their ends.
There are 2 independent parts, one for each index of `groups`. The reference program is written for one: setup_inputs(seed, part) draws one part's arguments, and reference() takes and returns one part's arrays. A program takes and returns all parts, laid end to end along the dimension named above; each array names one. Nothing has to cross between parts.
Inputs may be any that keep to these rules, and one draw needn't show every extreme that they name: `selection`: each row names 2 blocks that lie on 2 different indices of seq: the values block // 4 of a row are distinct. Every row names block 15.
All inputs are finite; a program needn't handle non-finite values.
Results may differ from the reference program's by a relative error of at most 0.0033.
Values may be sent and summed in bfloat16 or wider, within the bound.
No kernel may reach another device: no remote copies, remote signals or barrier semaphores. Data moves between devices by JAX's collectives and lax.ppermute only.
A program may use at most 64 MiB of HBM per device.

```python
import jax
import jax.numpy as jnp
from jax import lax

H = 64
HD = 128
TOK_SEQ = 384
BLOCK = 64
BLK_DEV = 4
F = 8192
SPAN = 1536
NBLK = 16
TOPK = 2
N_SEQ = 4


def shared_rows(key):
    base_q = jax.random.truncated_normal(jax.random.fold_in(key, 11), -4.0, 4.0, (SPAN, H * HD), jnp.float32)
    base_k = jax.random.truncated_normal(jax.random.fold_in(key, 12), -4.0, 4.0, (SPAN, H * HD), jnp.float32)
    return (base_q, base_k)


def draw_queries(key, part):
    base_q, base_k = shared_rows(key)
    result = 2.0 * base_q
    return result.astype(jnp.bfloat16)


def draw_new_keys(key, part):
    base_q, base_k = shared_rows(key)
    result = base_k
    return result.astype(jnp.bfloat16)


def draw_selection(key, part):
    hotness = jax.random.randint(jax.random.fold_in(key, 21), (N_SEQ,), 0, 4)
    hotness = hotness.at[N_SEQ - 1].set(6)
    noise = jax.random.randint(jax.random.fold_in(key, 22), (N_SEQ, N_SEQ), 0, 1 << 20)
    ranking = (hotness[None, :] * (1 << 20) + noise) * N_SEQ + jnp.arange(N_SEQ, dtype=jnp.int32)[None, :]
    unused, owners = lax.top_k(ranking, TOPK)
    inner = jax.random.randint(jax.random.fold_in(key, 23), (N_SEQ, TOPK), 0, BLK_DEV)
    inner = jnp.where(owners == N_SEQ - 1, BLK_DEV - 1, inner)
    return (owners * BLK_DEV + inner).astype(jnp.int32)


def steps_of(stream_key, shape, cuts, low, high):
    loudness = 1.0
    for axis_at, blocks in cuts:
        draws = jax.random.uniform(jax.random.fold_in(jax.random.fold_in(stream_key, 6), axis_at), (blocks,), jnp.float32, low / len(cuts), high / len(cuts))
        loudness = loudness * jnp.repeat(jnp.exp(draws), shape[axis_at] // blocks).reshape((-1,) + (1,) * (len(shape) - 1 - axis_at))
    return loudness


def normal_values(rng, shape, scale, bound, cuts=(), held_as=jnp.bfloat16):
    values = jax.random.normal(rng, shape, jnp.float32) * scale
    if len(cuts) > 0:
        values = steps_of(rng, shape, cuts, -0.22, 0.18) * values
    return jnp.clip(values, min=-bound, max=bound).astype(held_as)


def setup_inputs(seed: int = 0, part: int = 0) -> dict:
    splits = jax.random.split(jax.random.key(seed), 7)
    part_splits = jax.random.split(jax.random.fold_in(splits[6], part), 7)
    queries = draw_queries(jax.random.fold_in(jax.random.fold_in(splits[6], part), 71), part)
    new_keys = draw_new_keys(jax.random.fold_in(jax.random.fold_in(splits[6], part), 71), part)
    new_values = normal_values(part_splits[2], (SPAN, F), 1.0, 6.0, ((0, 16),))
    key_cache = normal_values(part_splits[3], (NBLK * BLOCK, F), 1.0, 6.0, ((0, 4), (1, 4)))
    value_cache = normal_values(part_splits[4], (NBLK * BLOCK, F), 1.0, 6.0, ((0, 4), (1, 4)))
    selection = draw_selection(jax.random.fold_in(jax.random.fold_in(splits[6], part), 71), part)
    return {"queries": queries, "new_keys": new_keys, "new_values": new_values, "key_cache": key_cache, "value_cache": value_cache, "selection": selection}


def reference(queries, new_keys, new_values, key_cache, value_cache, selection):
    scale = float(HD) ** -0.5
    cached_k = key_cache.reshape(NBLK, BLOCK, H, HD)
    cached_v = value_cache.reshape(NBLK, BLOCK, H, HD)
    query_blocks = queries.reshape(N_SEQ, TOK_SEQ, H, HD)
    key_blocks = new_keys.reshape(N_SEQ, TOK_SEQ, H, HD)
    value_blocks = new_values.reshape(N_SEQ, TOK_SEQ, H, HD)
    causal = jnp.arange(TOK_SEQ)[:, None] >= jnp.arange(TOK_SEQ)[None, :]
    visible = jnp.concatenate([jnp.ones((TOK_SEQ, TOPK * BLOCK), dtype=bool), causal], axis=1)

    def one_block(items):
        query_rows, key_rows, value_rows, picks = items
        picks = picks.astype(jnp.int32)
        remote_k = cached_k[picks].reshape(TOPK * BLOCK, H, HD)
        remote_v = cached_v[picks].reshape(TOPK * BLOCK, H, HD)
        all_keys = jnp.concatenate([remote_k, key_rows], axis=0).astype(jnp.float32)
        all_values = jnp.concatenate([remote_v, value_rows], axis=0).astype(jnp.float32)
        scores = jnp.einsum('thd,khd->htk', query_rows.astype(jnp.float32), all_keys) * scale
        scores = jnp.where(visible[None], scores, jnp.float32(-1e30))
        top = jnp.max(scores, axis=-1, keepdims=True)
        weights = jnp.exp(scores - top)
        total = jnp.sum(weights, axis=-1, keepdims=True)
        rounded = lax.optimization_barrier(weights.astype(jnp.bfloat16)).astype(jnp.float32)
        mixed = jnp.einsum('htk,khd->thd', rounded, all_values)
        mixed = mixed / jnp.transpose(total, (1, 0, 2))
        return mixed.astype(jnp.bfloat16).reshape(TOK_SEQ, H * HD)

    result = lax.map(one_block, (query_blocks, key_blocks, value_blocks, selection))
    return result.reshape(SPAN, H * HD)
```

```python
import functools

import jax
import jax.numpy as jnp
from jax import lax
from jax.experimental import pallas as pl
from jax.experimental.pallas import tpu as pltpu
from jax.sharding import PartitionSpec as P

HD = 128
BLOCK = 64
LOG2E = 1.4426950408889634
MASKED = -1e30


def softmax_rows(scores, values):
    top = functools.reduce(jnp.maximum, [jnp.max(s, axis=1, keepdims=True) for s in scores])
    weights = [jnp.exp2(s - top) for s in scores]
    total = functools.reduce(jnp.add, [jnp.sum(w, axis=1, keepdims=True) for w in weights])
    mixed = functools.reduce(
        jnp.add,
        [
            jnp.dot(w.astype(jnp.bfloat16), v, preferred_element_type=jnp.float32)
            for w, v in zip(weights, values)
        ],
    )
    return mixed, top, total


def logits(q, k, factor):
    return lax.dot_general(
        q, k, (((1,), (1,)), ((), ())), preferred_element_type=jnp.float32
    ) * factor


def ulysses_kernel(n, topk, per, parts, factor, where_ref, own_ref, *refs):
    qs, ks, vs = refs[:n], refs[n : 2 * n], refs[2 * n : 3 * n]
    cks, cvs = refs[3 * n : 3 * n + topk], refs[3 * n + topk : 3 * n + 2 * topk]
    out_ref, q_all, k_all, v_all = refs[3 * n + 2 * topk :]
    rows = qs[0].shape[0]
    count = rows * n
    for b in range(n):
        at = pl.ds(pl.multiple_of(where_ref[1 + b] * rows, rows), rows)
        q_all[at, :] = qs[b][...]
        k_all[at, :] = ks[b][...]
        v_all[at, :] = vs[b][...]
    step = count // parts
    causal = lax.broadcasted_iota(jnp.int32, (step, step), 0) >= lax.broadcasted_iota(
        jnp.int32, (step, step), 1
    )
    for j in range(per):
        col = slice(j * HD, (j + 1) * HD)
        ck = [r[0, :, col] for r in cks]
        cv = [r[0, :, col] for r in cvs]
        ck = jnp.concatenate(ck, axis=0)
        cv = jnp.concatenate(cv, axis=0)
        for i in range(parts):
            here = slice(i * step, (i + 1) * step)
            q = q_all[here, col]
            scores = [logits(q, ck, factor)]
            values = [cv]
            if i > 0:
                scores.append(logits(q, k_all[: i * step, col], factor))
                values.append(v_all[: i * step, col])
            scores.append(jnp.where(causal, logits(q, k_all[here, col], factor), MASKED))
            values.append(v_all[here, col])
            mixed, top, total = softmax_rows(scores, values)
            out_ref[here, col] = (mixed / total).astype(jnp.bfloat16)


def ulysses(n, subs, queries, new_keys, new_values, key_cache, value_cache, selection):
    rows, features = queries.shape
    width = features // n
    heads = width // HD
    topk = selection.shape[1]
    me = lax.axis_index("seq")
    group = lax.axis_index("head") * subs + lax.axis_index("sub")

    def peer(b):
        return lax.rem(group + b, n)

    def exchange(b, piece):
        return lax.ppermute(piece, ("head", "sub"), [(i, (i + b) % n) for i in range(n)])

    def spread(array):
        pieces = [array]
        for b in range(1, n):
            piece = lax.dynamic_slice_in_dim(array, peer(b) * width, width, axis=1)
            pieces.append(exchange(b, piece))
        return pieces

    blk_dev = key_cache.shape[0] // BLOCK
    owner_of = selection // blk_dev
    inner = jnp.sum(jnp.where(owner_of == me, selection % blk_dev, 0), axis=1)
    mine = lax.dynamic_index_in_dim(selection, me, 0, keepdims=False) // blk_dev
    got = [
        lax.all_to_all(
            cache.reshape(blk_dev, BLOCK, -1)[inner], "seq", split_axis=0, concat_axis=0, tiled=True
        )
        for cache in (key_cache, value_cache)
    ]
    q_pieces, k_pieces, v_pieces = spread(queries), spread(new_keys), spread(new_values)
    from_of = jnp.stack([group] + [lax.rem(group + b, n) for b in range(n, 0, -1)]).astype(jnp.int32)
    per = 2 if heads % 2 == 0 else 1
    cols = per * HD
    own = pl.BlockSpec((rows, cols), lambda h, w, o: (0, w[0] * (heads // per) + h))
    other = pl.BlockSpec((rows, cols), lambda h, w, o: (0, h))
    cached = [
        pl.BlockSpec((1, BLOCK, cols), functools.partial(lambda t, h, w, o: (o[t], 0, h), t))
        for t in range(topk)
    ]
    count = rows * n
    out = pl.pallas_call(
        functools.partial(
            ulysses_kernel, n, topk, per, 2, float(HD) ** (-0.5) * LOG2E
        ),
        out_shape=jax.ShapeDtypeStruct((count, width), jnp.bfloat16),
        grid_spec=pltpu.PrefetchScalarGridSpec(
            num_scalar_prefetch=2,
            grid=(heads // per,),
            in_specs=([own] + [other] * (n - 1)) * 3 + cached * 2,
            out_specs=pl.BlockSpec((count, cols), lambda h, w, o: (0, h)),
            scratch_shapes=[pltpu.VMEM((count, cols), jnp.bfloat16)] * 3,
        ),
        name="attend",
    )(from_of, mine, *q_pieces, *k_pieces, *v_pieces, *([got[0]] * topk), *([got[1]] * topk))
    result = jnp.zeros((rows, features), jnp.bfloat16)
    for b in range(n):
        piece = lax.dynamic_slice_in_dim(out, peer(b) * rows, rows, axis=0)
        if b > 0:
            piece = exchange(b, piece)
        result = lax.dynamic_update_slice_in_dim(
            result, piece, lax.rem(group + n - b, n) * width, axis=1
        )
    return result


def solution(mesh):
    subs = mesh.shape["sub"]
    n = mesh.shape["head"] * subs
    placed = (
        P(("groups", "seq", "head", "sub"), None),
        P(("groups", "seq", "head", "sub"), None),
        P(("groups", "seq", "head", "sub"), None),
        P(("groups", "seq"), ("head", "sub")),
        P(("groups", "seq"), ("head", "sub")),
        P("groups", None),
    )
    return jax.shard_map(
        functools.partial(ulysses, n, subs),
        mesh=mesh,
        in_specs=placed,
        out_specs=P(("groups", "seq", "head", "sub"), None),
        check_vma=False,
    )
```

```python
import functools

import jax
import jax.numpy as jnp
from jax import lax
from jax.experimental import pallas as pl
from jax.experimental.pallas import tpu as pltpu
from jax.sharding import PartitionSpec as P

HD = 128
BLOCK = 64
LOG2E = 1.4426950408889634
MASKED = -1e30


def softmax_rows(scores, values):
    top = functools.reduce(jnp.maximum, [jnp.max(s, axis=1, keepdims=True) for s in scores])
    weights = [jnp.exp2(s - top) for s in scores]
    total = functools.reduce(jnp.add, [jnp.sum(w, axis=1, keepdims=True) for w in weights])
    mixed = functools.reduce(
        jnp.add,
        [
            jnp.dot(w.astype(jnp.bfloat16), v, preferred_element_type=jnp.float32)
            for w, v in zip(weights, values)
        ],
    )
    return mixed, top, total


def logits(q, k, factor):
    return lax.dot_general(
        q, k, (((1,), (1,)), ((), ())), preferred_element_type=jnp.float32
    ) * factor


def ulysses_kernel(n, topk, per, parts, factor, where_ref, own_ref, *refs):
    qs, ks, vs = refs[:n], refs[n : 2 * n], refs[2 * n : 3 * n]
    cks, cvs = refs[3 * n : 3 * n + topk], refs[3 * n + topk : 3 * n + 2 * topk]
    out_ref, q_all, k_all, v_all = refs[3 * n + 2 * topk :]
    rows = qs[0].shape[0]
    count = rows * n
    for b in range(n):
        at = pl.ds(pl.multiple_of(where_ref[1 + b] * rows, rows), rows)
        q_all[at, :] = qs[b][...]
        k_all[at, :] = ks[b][...]
        v_all[at, :] = vs[b][...]
    step = count // parts
    causal = lax.broadcasted_iota(jnp.int32, (step, step), 0) >= lax.broadcasted_iota(
        jnp.int32, (step, step), 1
    )
    for j in range(per):
        col = slice(j * HD, (j + 1) * HD)
        ck = [r[0, :, col] for r in cks]
        cv = [r[0, :, col] for r in cvs]
        ck = jnp.concatenate(ck, axis=0)
        cv = jnp.concatenate(cv, axis=0)
        for i in range(parts):
            here = slice(i * step, (i + 1) * step)
            q = q_all[here, col]
            scores = [logits(q, ck, factor)]
            values = [cv]
            if i > 0:
                scores.append(logits(q, k_all[: i * step, col], factor))
                values.append(v_all[: i * step, col])
            scores.append(jnp.where(causal, logits(q, k_all[here, col], factor), MASKED))
            values.append(v_all[here, col])
            mixed, top, total = softmax_rows(scores, values)
            out_ref[here, col] = (mixed / total).astype(jnp.bfloat16)


def ulysses(n, subs, queries, new_keys, new_values, key_cache, value_cache, selection):
    rows, features = queries.shape
    width = features // n
    heads = width // HD
    topk = selection.shape[1]
    me = lax.axis_index("seq")
    group = lax.axis_index("head") * subs + lax.axis_index("sub")

    def peer(b):
        return lax.rem(group + b, n)

    def exchange(b, piece):
        return lax.ppermute(piece, ("head", "sub"), [(i, (i + b) % n) for i in range(n)])

    def spread(array):
        pieces = [array]
        for b in range(1, n):
            piece = lax.dynamic_slice_in_dim(array, peer(b) * width, width, axis=1)
            pieces.append(exchange(b, piece))
        return pieces

    blk_dev = key_cache.shape[0] // BLOCK
    owner_of = selection // blk_dev
    inner = jnp.sum(jnp.where(owner_of == me, selection % blk_dev, 0), axis=1)
    mine = lax.dynamic_index_in_dim(selection, me, 0, keepdims=False) // blk_dev
    got = [
        lax.all_to_all(
            cache.reshape(blk_dev, BLOCK, -1)[inner], "seq", split_axis=0, concat_axis=0, tiled=True
        )
        for cache in (key_cache, value_cache)
    ]
    q_pieces, k_pieces, v_pieces = spread(queries), spread(new_keys), spread(new_values)
    from_of = jnp.stack([group] + [lax.rem(group + b, n) for b in range(n, 0, -1)]).astype(jnp.int32)
    per = 2 if heads % 2 == 0 else 1
    cols = per * HD
    own = pl.BlockSpec((rows, cols), lambda h, w, o: (0, w[0] * (heads // per) + h))
    other = pl.BlockSpec((rows, cols), lambda h, w, o: (0, h))
    cached = [
        pl.BlockSpec((1, BLOCK, cols), functools.partial(lambda t, h, w, o: (o[t], 0, h), t))
        for t in range(topk)
    ]
    count = rows * n
    out = pl.pallas_call(
        functools.partial(
            ulysses_kernel, n, topk, per, 2, float(HD) ** (-0.5) * LOG2E
        ),
        out_shape=jax.ShapeDtypeStruct((count, width), jnp.bfloat16),
        grid_spec=pltpu.PrefetchScalarGridSpec(
            num_scalar_prefetch=2,
            grid=(heads // per,),
            in_specs=([own] + [other] * (n - 1)) * 3 + cached * 2,
            out_specs=pl.BlockSpec((count, cols), lambda h, w, o: (0, h)),
            scratch_shapes=[pltpu.VMEM((count, cols), jnp.bfloat16)] * 3,
        ),
        name="attend",
    )(from_of, mine, *q_pieces, *k_pieces, *v_pieces, *([got[0]] * topk), *([got[1]] * topk))
    result = jnp.zeros((rows, features), jnp.bfloat16)
    for b in range(n):
        piece = lax.dynamic_slice_in_dim(out, peer(b) * rows, rows, axis=0)
        if b > 0:
            piece = exchange(b, piece)
        result = lax.dynamic_update_slice_in_dim(
            result, piece, lax.rem(group + n - b, n) * width, axis=1
        )
    return result


def ordered(own_ref, par_ref, place, rows, cols, into):
    at = pl.ds(pl.multiple_of(place * rows, rows), rows)
    into[at, :] = own_ref[:, cols]
    at = pl.ds(pl.multiple_of((1 - place) * rows, rows), rows)
    into[at, :] = par_ref[:, cols]


def causal_mask(size):
    return lax.broadcasted_iota(jnp.int32, (size, size), 0) >= lax.broadcasted_iota(
        jnp.int32, (size, size), 1
    )


def lane_put(into, lane, column):
    lanes = lax.broadcasted_iota(jnp.int32, into.shape, 1)
    return jnp.where(lanes == lane, column, into)


def early_kernel(
    per, steps, factor, at_ref, qo, qp, ko, kp, vo, vp, xo, xp, ob, lb, loc, part, stat, qs, ks, vs, xs
):
    rows = qo.shape[0]
    chip_rows = 2 * rows
    place = at_ref[0]
    h = pl.program_id(0)
    causal = causal_mask(chip_rows)

    @pl.when(h == 0)
    def _():
        stat[...] = jnp.zeros_like(stat)

    for j in range(per):
        col = slice(j * HD, (j + 1) * HD)
        ordered(qo, qp, place, rows, col, qs)
        ordered(ko, kp, place, rows, col, ks)
        ordered(vo, vp, place, rows, col, vs)
        out_at = pl.ds(pl.multiple_of((h * per + j) * HD, HD), HD)
        lane = (h * per + j) * 2

        @pl.when(at_ref[1] == 0)
        def _():
            ordered(xo, xp, place, rows, col, xs)
            ck = jnp.concatenate([ob[:BLOCK, col], lb[:BLOCK, col]], axis=0)
            cv = jnp.concatenate([ob[BLOCK:, col], lb[BLOCK:, col]], axis=0)
            q = qs[...]
            scores = [
                logits(q, ck, factor),
                jnp.where(causal, logits(q, ks[...], factor), MASKED),
            ]
            mixed, top, total = softmax_rows(scores, [cv, vs[...]])
            loc[:, col] = mixed / total
            q = xs[...]
            scores = [logits(q, ck, factor), logits(q, ks[...], factor)]
            mixed, top, total = softmax_rows(scores, [cv, vs[...]])
            part[:, out_at] = (mixed / total).astype(jnp.bfloat16)
            stat[...] = lane_put(lane_put(stat[...], lane, top), lane + 1, total)

        @pl.when(at_ref[1] == 1)
        def _():
            scores = [jnp.where(causal, logits(qs[...], ks[...], factor), MASKED)]
            mixed, top, total = softmax_rows(scores, [vs[...]])
            loc[:, col] = mixed
            stat[...] = lane_put(lane_put(stat[...], lane, top), lane + 1, total)

    @pl.when((h == steps - 1) & (at_ref[1] == 0))
    def _():
        whole = stat[...]
        packed = jnp.zeros_like(whole)
        for t in range(3):
            piece = whole.astype(jnp.bfloat16).astype(jnp.float32)
            whole = whole - piece
            packed = packed + (pltpu.roll(piece, t * STATS, 1) if t > 0 else piece)
        part[:, steps * per * HD :] = packed.astype(jnp.bfloat16)


def late_kernel(
    per, factor, at_ref, qo, qp, ko, kp, vo, vp, xo, xp, yo, yp, ob, lb, cx, out, qs, ks, vs, xs, ys
):
    rows = qo.shape[0]
    place = at_ref[0]
    causal = causal_mask(2 * rows)
    for j in range(per):
        col = slice(j * HD, (j + 1) * HD)
        ordered(qo, qp, place, rows, col, qs)
        ordered(ko, kp, place, rows, col, ks)
        ordered(vo, vp, place, rows, col, vs)

        def finish(scores, values):
            mixed, top, total = softmax_rows(scores, values)
            out[:, col] = (mixed / total).astype(jnp.bfloat16)

        @pl.when(at_ref[1] == 0)
        def _():
            q = qs[...]
            ck = jnp.concatenate([cx[:BLOCK, col], cx[2 * BLOCK : 3 * BLOCK, col]], axis=0)
            cv = jnp.concatenate([cx[BLOCK : 2 * BLOCK, col], cx[3 * BLOCK :, col]], axis=0)
            scores = [
                logits(q, ck, factor),
                jnp.where(causal, logits(q, ks[...], factor), MASKED),
            ]
            finish(scores, [cv, vs[...]])

        @pl.when(at_ref[1] == 1)
        def _():
            ordered(xo, xp, place, rows, col, xs)
            ordered(yo, yp, place, rows, col, ys)
            q = qs[...]
            ck = jnp.concatenate([ob[:BLOCK, col], lb[:BLOCK, col]], axis=0)
            cv = jnp.concatenate([ob[BLOCK:, col], lb[BLOCK:, col]], axis=0)
            scores = [
                logits(q, ck, factor),
                logits(q, xs[...], factor),
                jnp.where(causal, logits(q, ks[...], factor), MASKED),
            ]
            finish(scores, [cv, ys[...], vs[...]])


def merge_kernel(heads, at_ref, loc, stat, far, out):
    @pl.when(at_ref[1] == 0)
    def _():
        out[...] = loc[...].astype(jnp.bfloat16)

    @pl.when(at_ref[1] == 1)
    def _():
        packed = far[:, heads * HD :].astype(jnp.float32)
        lanes = packed.shape[1]
        there = packed
        for t in range(1, 3):
            there = there + pltpu.roll(packed, lanes - t * STATS, 1)
        here = stat[...]
        for i in range(heads):
            col = slice(i * HD, (i + 1) * HD)
            near_top, near_sum = here[:, 2 * i : 2 * i + 1], here[:, 2 * i + 1 : 2 * i + 2]
            far_top, far_sum = there[:, 2 * i : 2 * i + 1], there[:, 2 * i + 1 : 2 * i + 2]
            top = jnp.maximum(near_top, far_top)
            near = jnp.exp2(near_top - top)
            away = far_sum * jnp.exp2(far_top - top)
            mixed = loc[:, col] * near + far[:, col].astype(jnp.float32) * away
            out[:, col] = (mixed / (near_sum * near + away)).astype(jnp.bfloat16)


def assemble_kernel(width, at_ref, *refs):
    outs, gots, result = refs[:4], refs[4:8], refs[8]
    rows = result.shape[0]
    place = at_ref[0]
    for g in range(2):
        for j in range(2):
            half = width // 2
            own, got = outs[2 * g + j], gots[2 * g + j]
            base = g * 2 * width + j * half
            here = pl.ds(pl.multiple_of(place * rows, rows), rows)
            to = pl.ds(pl.multiple_of(base + place * width, half), half)
            result[:, to] = own[here, :]
            to = pl.ds(pl.multiple_of(base + (1 - place) * width, half), half)
            result[:, to] = got[...]


STATS = 16
DOWN = ((3, 2, 3, 0), ((0, 1), (1, 2), (2, 3)))
UP = ((0, 0, 1, 2), ((3, 2), (2, 1), (1, 0)))
FAR = ((2, 0, 0, 1), ((3, 1), (2, 0), (0, 2)))
MERGED = ((1, 3, 0, 0), ((0, 1), (1, 3)))
LAST = ((1, 0),)
OTHER_FROM = ((0, 2, 3), (4, 0, 2), (3, 1, 0), (4, 4, 1))
LAST_FROM = (5, 3, 2, 0)


def hybrid(queries, new_keys, new_values, key_cache, value_cache, selection):
    rows, features = queries.shape
    width = features // 4
    half = width // 2
    heads = width // HD
    half_heads = heads // 2
    me = lax.axis_index("seq")
    r = lax.axis_index("head")
    c = lax.axis_index("sub")
    at = jnp.stack([c, r]).astype(jnp.int32)
    factor = float(HD) ** (-0.5) * LOG2E

    def to_partner(x):
        return lax.ppermute(x, "sub", [(0, 1), (1, 0)])

    def across(x, pairs=((0, 1), (1, 0))):
        return lax.ppermute(x, "head", list(pairs))

    def column(x, block):
        return lax.dynamic_slice_in_dim(x, block * width, width, axis=1)

    blk_dev = key_cache.shape[0] // BLOCK
    n_seq = selection.shape[0]
    owner = selection // blk_dev
    inner_for = jnp.sum(jnp.where(owner == me, selection % blk_dev, 0), axis=1)
    from_me = jnp.any(owner == me, axis=1)
    my_owner = jnp.sum(
        jnp.where(owner == n_seq - 1, 0, owner), axis=1
    )[me]
    other_from = jnp.array(OTHER_FROM, jnp.int32)[me, my_owner]
    last_from = jnp.array(LAST_FROM, jnp.int32)[me]

    def block(row, j):
        start = (inner_for[row] * BLOCK, j * half)
        return jnp.concatenate(
            [
                lax.dynamic_slice(key_cache, start, (BLOCK, half)),
                lax.dynamic_slice(value_cache, start, (BLOCK, half)),
            ],
            axis=0,
        )

    def row_of(table):
        return jnp.array(table, jnp.int32)[me]

    def along(x, pairs):
        return lax.ppermute(x, "seq", list(pairs))

    def fetch(j):
        own = block(me, j)
        with jax.named_scope(f"down{j}"):
            down = along(block(row_of(DOWN[0]), j), DOWN[1])
        with jax.named_scope(f"up{j}"):
            up = along(block(row_of(UP[0]), j), UP[1])
        with jax.named_scope(f"far{j}"):
            far = along(block(row_of(FAR[0]), j), FAR[1])
        relay = (me == 1) & ~from_me[3]
        with jax.named_scope(f"merged{j}"):
            merged = along(jnp.where(relay, down, block(row_of(MERGED[0]), j)), MERGED[1])
        with jax.named_scope(f"last{j}"):
            last = along(far, LAST)
        def pick(code, options):
            result = options[0][1]
            for value, array in options[1:]:
                result = jnp.where(code == value, array, result)
            return result

        other = pick(other_from, [(0, own), (1, down), (2, up), (3, far), (4, merged)])
        final = pick(last_from, [(0, own), (2, up), (3, far), (5, last)])
        return other, final

    first_half = fetch(0)

    def swapped(x):
        pieces = x.reshape(rows, 2, 2, width)
        piece = lax.dynamic_slice(pieces, (0, 0, 1 - c, 0), (rows, 2, 1, width))
        return to_partner(piece.reshape(rows, 2 * width))

    with jax.named_scope("x_own"):
        x_own = across(jnp.where(r == 0, column(new_keys, 2 + c), column(queries, c)))
    with jax.named_scope("swap_k"):
        k_par = swapped(new_keys)
    with jax.named_scope("swap_q"):
        q_par = swapped(queries)
    with jax.named_scope("x_par"):
        x_par = across(jnp.where(r == 0, k_par[:, width:], q_par[:, :width]))
    with jax.named_scope("y_own"):
        y_own = across(column(new_values, 2 + c), ((0, 1),))
    with jax.named_scope("swap_v"):
        v_par = swapped(new_values)
    with jax.named_scope("y_par"):
        y_par = across(v_par[:, width:], ((0, 1),))

    second_half = fetch(1)
    per = 2
    steps = half_heads // per
    cols = per * HD
    blocks = heads // per

    def early(j, cache):
        own = pl.BlockSpec((rows, cols), lambda h, a: (0, a[0] * blocks + j * steps + h))
        par = pl.BlockSpec((rows, cols), lambda h, a: (0, j * steps + h))
        kept = pl.BlockSpec((2 * BLOCK, cols), lambda h, a: (0, h))
        return pl.pallas_call(
            functools.partial(early_kernel, per, steps, factor),
            out_shape=(
                jax.ShapeDtypeStruct((2 * rows, half), jnp.float32),
                jax.ShapeDtypeStruct((2 * rows, half + HD), jnp.bfloat16),
                jax.ShapeDtypeStruct((2 * rows, HD), jnp.float32),
            ),
            grid_spec=pltpu.PrefetchScalarGridSpec(
                num_scalar_prefetch=1,
                grid=(steps,),
                in_specs=[own, par] * 3 + [par, par, kept, kept],
                out_specs=[
                    pl.BlockSpec((2 * rows, cols), lambda h, a: (0, h)),
                    pl.BlockSpec((2 * rows, half + HD), lambda h, a: (0, 0)),
                    pl.BlockSpec((2 * rows, HD), lambda h, a: (0, 0)),
                ],
                scratch_shapes=[pltpu.VMEM((2 * rows, HD), jnp.bfloat16)] * 4,
            ),
            name=f"early{j}",
        )(at, queries, q_par, new_keys, k_par, new_values, v_par, x_own, x_par, *cache)

    def late(j, cache, crossed):
        own = pl.BlockSpec((rows, cols), lambda h, a: (0, (2 + a[0]) * blocks + j * steps + h))
        par = pl.BlockSpec((rows, cols), lambda h, a: (0, blocks + j * steps + h))
        sent = pl.BlockSpec((rows, cols), lambda h, a: (0, j * steps + h))
        kept = pl.BlockSpec((2 * BLOCK, cols), lambda h, a: (0, h))
        both = pl.BlockSpec((4 * BLOCK, cols), lambda h, a: (0, h))
        return pl.pallas_call(
            functools.partial(late_kernel, per, factor),
            out_shape=jax.ShapeDtypeStruct((2 * rows, half), jnp.bfloat16),
            grid_spec=pltpu.PrefetchScalarGridSpec(
                num_scalar_prefetch=1,
                grid=(steps,),
                in_specs=[own, par] * 3 + [sent] * 4 + [kept, kept, both],
                out_specs=pl.BlockSpec((2 * rows, cols), lambda h, a: (0, h)),
                scratch_shapes=[pltpu.VMEM((2 * rows, HD), jnp.bfloat16)] * 5,
            ),
            name=f"late{j}",
        )(
            at, queries, q_par, new_keys, k_par, new_values, v_par,
            x_own, x_par, y_own, y_par, *cache, crossed,
        )

    def merge(j, loc, stat, far):
        return pl.pallas_call(
            functools.partial(merge_kernel, half_heads),
            out_shape=jax.ShapeDtypeStruct((2 * rows, half), jnp.bfloat16),
            grid_spec=pltpu.PrefetchScalarGridSpec(
                num_scalar_prefetch=1,
                grid=(1,),
                in_specs=[
                    pl.BlockSpec(x.shape, lambda h, a: (0, 0)) for x in (loc, stat, far)
                ],
                out_specs=pl.BlockSpec((2 * rows, half), lambda h, a: (0, 0)),
            ),
            name=f"merge{j}",
        )(at, loc, stat, far)

    def give(out):
        return to_partner(lax.dynamic_slice_in_dim(out, (1 - c) * rows, rows, axis=0))

    outs, gots = [None] * 4, [None] * 4
    with jax.named_scope("cache0"):
        crossed0 = across(jnp.concatenate(first_half, axis=0), ((1, 0),))
    loc0, part0, stat0 = early(0, first_half)
    with jax.named_scope("part0"):
        far0 = across(part0, ((0, 1),))
    with jax.named_scope("cache1"):
        crossed1 = across(jnp.concatenate(second_half, axis=0), ((1, 0),))
    loc1, part1, stat1 = early(1, second_half)
    with jax.named_scope("part1"):
        far1 = across(part1, ((0, 1),))
    outs[2] = late(0, first_half, crossed0)
    with jax.named_scope("give2"):
        gots[2] = give(outs[2])
    outs[3] = late(1, second_half, crossed1)
    with jax.named_scope("give3"):
        gots[3] = give(outs[3])
    outs[0] = merge(0, loc0, stat0, far0)
    with jax.named_scope("give0"):
        gots[0] = give(outs[0])
    outs[1] = merge(1, loc1, stat1, far1)
    with jax.named_scope("give1"):
        gots[1] = give(outs[1])
    return pl.pallas_call(
        functools.partial(assemble_kernel, width),
        out_shape=jax.ShapeDtypeStruct((rows, features), jnp.bfloat16),
        grid_spec=pltpu.PrefetchScalarGridSpec(
            num_scalar_prefetch=1,
            grid=(1,),
            in_specs=[pl.BlockSpec(x.shape, lambda h, a: (0, 0)) for x in outs + gots],
            out_specs=pl.BlockSpec((rows, features), lambda h, a: (0, 0)),
        ),
        name="assemble",
    )(at, *outs, *gots)


def solution(mesh):
    subs = mesh.shape["sub"]
    n = mesh.shape["head"] * subs
    placed = (
        P(("groups", "seq", "head", "sub"), None),
        P(("groups", "seq", "head", "sub"), None),
        P(("groups", "seq", "head", "sub"), None),
        P(("groups", "seq"), ("head", "sub")),
        P(("groups", "seq"), ("head", "sub")),
        P("groups", None),
    )
    body = functools.partial(ulysses, n, subs)
    if (mesh.shape["head"], subs, mesh.shape["seq"]) == (2, 2, 4):
        body = hybrid

    return jax.shard_map(
        body,
        mesh=mesh,
        in_specs=placed,
        out_specs=P(("groups", "seq", "head", "sub"), None),
        check_vma=False,
    )
```

```python
import functools

import jax
import jax.numpy as jnp
from jax import lax
from jax.experimental import pallas as pl
from jax.experimental.pallas import tpu as pltpu
from jax.sharding import PartitionSpec as P

HD = 128
BLOCK = 64
LOG2E = 1.4426950408889634
MASKED = -1e30


def softmax_rows(scores, values):
    top = functools.reduce(jnp.maximum, [jnp.max(s, axis=1, keepdims=True) for s in scores])
    weights = [jnp.exp2(s - top) for s in scores]
    total = functools.reduce(jnp.add, [jnp.sum(w, axis=1, keepdims=True) for w in weights])
    mixed = functools.reduce(
        jnp.add,
        [
            jnp.dot(w.astype(jnp.bfloat16), v, preferred_element_type=jnp.float32)
            for w, v in zip(weights, values)
        ],
    )
    return mixed, top, total


def logits(q, k, factor):
    return lax.dot_general(
        q, k, (((1,), (1,)), ((), ())), preferred_element_type=jnp.float32
    ) * factor


def ulysses_kernel(n, topk, per, parts, factor, where_ref, own_ref, *refs):
    qs, ks, vs = refs[:n], refs[n : 2 * n], refs[2 * n : 3 * n]
    cks, cvs = refs[3 * n : 3 * n + topk], refs[3 * n + topk : 3 * n + 2 * topk]
    out_ref, q_all, k_all, v_all = refs[3 * n + 2 * topk :]
    rows = qs[0].shape[0]
    count = rows * n
    for b in range(n):
        at = pl.ds(pl.multiple_of(where_ref[1 + b] * rows, rows), rows)
        q_all[at, :] = qs[b][...]
        k_all[at, :] = ks[b][...]
        v_all[at, :] = vs[b][...]
    step = count // parts
    causal = lax.broadcasted_iota(jnp.int32, (step, step), 0) >= lax.broadcasted_iota(
        jnp.int32, (step, step), 1
    )
    for j in range(per):
        col = slice(j * HD, (j + 1) * HD)
        ck = [r[0, :, col] for r in cks]
        cv = [r[0, :, col] for r in cvs]
        ck = jnp.concatenate(ck, axis=0)
        cv = jnp.concatenate(cv, axis=0)
        for i in range(parts):
            here = slice(i * step, (i + 1) * step)
            q = q_all[here, col]
            scores = [logits(q, ck, factor)]
            values = [cv]
            if i > 0:
                scores.append(logits(q, k_all[: i * step, col], factor))
                values.append(v_all[: i * step, col])
            scores.append(jnp.where(causal, logits(q, k_all[here, col], factor), MASKED))
            values.append(v_all[here, col])
            mixed, top, total = softmax_rows(scores, values)
            out_ref[here, col] = (mixed / total).astype(jnp.bfloat16)


def ulysses(n, subs, queries, new_keys, new_values, key_cache, value_cache, selection):
    rows, features = queries.shape
    width = features // n
    heads = width // HD
    topk = selection.shape[1]
    me = lax.axis_index("seq")
    group = lax.axis_index("head") * subs + lax.axis_index("sub")

    def peer(b):
        return lax.rem(group + b, n)

    def exchange(b, piece):
        return lax.ppermute(piece, ("head", "sub"), [(i, (i + b) % n) for i in range(n)])

    def spread(array):
        pieces = [array]
        for b in range(1, n):
            piece = lax.dynamic_slice_in_dim(array, peer(b) * width, width, axis=1)
            pieces.append(exchange(b, piece))
        return pieces

    blk_dev = key_cache.shape[0] // BLOCK
    owner_of = selection // blk_dev
    inner = jnp.sum(jnp.where(owner_of == me, selection % blk_dev, 0), axis=1)
    mine = lax.dynamic_index_in_dim(selection, me, 0, keepdims=False) // blk_dev
    got = [
        lax.all_to_all(
            cache.reshape(blk_dev, BLOCK, -1)[inner], "seq", split_axis=0, concat_axis=0, tiled=True
        )
        for cache in (key_cache, value_cache)
    ]
    q_pieces, k_pieces, v_pieces = spread(queries), spread(new_keys), spread(new_values)
    from_of = jnp.stack([group] + [lax.rem(group + b, n) for b in range(n, 0, -1)]).astype(jnp.int32)
    per = 2 if heads % 2 == 0 else 1
    cols = per * HD
    own = pl.BlockSpec((rows, cols), lambda h, w, o: (0, w[0] * (heads // per) + h))
    other = pl.BlockSpec((rows, cols), lambda h, w, o: (0, h))
    cached = [
        pl.BlockSpec((1, BLOCK, cols), functools.partial(lambda t, h, w, o: (o[t], 0, h), t))
        for t in range(topk)
    ]
    count = rows * n
    out = pl.pallas_call(
        functools.partial(
            ulysses_kernel, n, topk, per, 2, float(HD) ** (-0.5) * LOG2E
        ),
        out_shape=jax.ShapeDtypeStruct((count, width), jnp.bfloat16),
        grid_spec=pltpu.PrefetchScalarGridSpec(
            num_scalar_prefetch=2,
            grid=(heads // per,),
            in_specs=([own] + [other] * (n - 1)) * 3 + cached * 2,
            out_specs=pl.BlockSpec((count, cols), lambda h, w, o: (0, h)),
            scratch_shapes=[pltpu.VMEM((count, cols), jnp.bfloat16)] * 3,
        ),
        name="attend",
    )(from_of, mine, *q_pieces, *k_pieces, *v_pieces, *([got[0]] * topk), *([got[1]] * topk))
    result = jnp.zeros((rows, features), jnp.bfloat16)
    for b in range(n):
        piece = lax.dynamic_slice_in_dim(out, peer(b) * rows, rows, axis=0)
        if b > 0:
            piece = exchange(b, piece)
        result = lax.dynamic_update_slice_in_dim(
            result, piece, lax.rem(group + n - b, n) * width, axis=1
        )
    return result


def chip_bias(bias, place, rows, visible):
    shape = (2 * rows, visible + 2 * rows)

    def token(at):
        return jnp.where(at < rows, place * rows + at, (1 - place) * rows + at - rows)

    q = token(lax.broadcasted_iota(jnp.int32, shape, 0))
    k = lax.broadcasted_iota(jnp.int32, shape, 1) - visible
    bias[...] = jnp.where((k < 0) | (q >= token(k)), 0.0, MASKED)


def soft(scores, values):
    top = jnp.max(scores, axis=1, keepdims=True)
    weights = jnp.exp2(scores - top)
    total = jnp.sum(weights, axis=1, keepdims=True)
    mixed = jnp.dot(weights.astype(jnp.bfloat16), values, preferred_element_type=jnp.float32)
    return (mixed * (1.0 / total)).astype(jnp.bfloat16)


def run_copies(pairs, sems):
    copies = [pltpu.make_async_copy(a, b, sems.at[i]) for i, (a, b) in enumerate(pairs)]
    for copy in copies:
        copy.start()
    for copy in copies:
        copy.wait()


def lookup(table, index):
    result = jnp.int32(table[0])
    for i in range(1, len(table)):
        result = jnp.where(index == i, jnp.int32(table[i]), result)
    return result


def held(sel_ref, row, owner, blk_dev):
    inner = jnp.int32(0)
    for t in range(sel_ref.shape[1]):
        picked = sel_ref[row, t]
        match = lax.div(picked, jnp.int32(blk_dev)) == owner
        inner = jnp.where(match, lax.rem(picked, jnp.int32(blk_dev)), inner)
    return inner


def pack_kernel(n, width, start, size, at_ref, q, k, v, after, *refs):
    outs, sems = refs[: n - 1], refs[n - 1]
    pairs = []
    for d in range(1, n):
        to = (at_ref[0] ^ d) * width + start
        cols = pl.ds(pl.multiple_of(to, HD), size)
        for i, array in enumerate((q, k, v)):
            pairs.append((array.at[:, cols], outs[d - 1].at[:, i * size : (i + 1) * size]))
    run_copies(pairs, sems)


def sends_kernel(n_seq, blk_dev, chunks, at_ref, sel_ref, kc, vc, after, *refs):
    outs, sems = refs[:-1], refs[-1]
    me = at_ref[1]
    pairs = []
    for i, (start, size) in enumerate(chunks):
        for d in range(1, n_seq):
            inner = held(sel_ref, me ^ d, me, blk_dev)
            at = pl.ds(pl.multiple_of(inner * BLOCK, BLOCK), BLOCK)
            to = outs[i * (n_seq - 1) + d - 1]
            pairs.append((kc.at[at, start : start + size], to.at[:BLOCK]))
            pairs.append((vc.at[at, start : start + size], to.at[BLOCK:]))
    run_copies(pairs, sems)


def attend_kernel(per, n_seq, blk_dev, start, size, factor, at_ref, sel_ref, *refs):
    own, sub, head, diag = refs[0:3], refs[3:6], refs[6:9], refs[9:12]
    kc, vc = refs[12:14]
    came = refs[14 : 14 + n_seq - 1]
    outs = refs[14 + n_seq - 1 : 18 + n_seq - 1]
    kept, near, bias, sems = refs[18 + n_seq - 1 :]
    rows = own[0].shape[0]
    h = pl.program_id(0)
    topk = sel_ref.shape[1]
    seen = topk * BLOCK

    @pl.when(h == 0)
    def _():
        me = at_ref[1]
        for t in range(topk):
            picked = sel_ref[me, t]
            owner = lax.div(picked, jnp.int32(blk_dev))
            inner = lax.rem(picked, jnp.int32(blk_dev))
            at = pl.ds(pl.multiple_of(inner * BLOCK, BLOCK), BLOCK)
            k_to = kept.at[t * BLOCK : (t + 1) * BLOCK]
            v_to = kept.at[seen + t * BLOCK : seen + (t + 1) * BLOCK]
            here = slice(start, start + size)
            sources = [(kc.at[at, here], vc.at[at, here])]
            sources += [(a.at[:BLOCK], a.at[BLOCK:]) for a in came]
            for d, (k_from, v_from) in enumerate(sources):

                @pl.when(owner ^ me == d)
                def _():
                    pltpu.make_async_copy(k_from, k_to, sems.at[2 * t]).start()
                    pltpu.make_async_copy(v_from, v_to, sems.at[2 * t + 1]).start()

        chip_bias(near, at_ref[3], rows, seen)
        chip_bias(bias, at_ref[3], rows, seen + 2 * rows)
        for t in range(topk):
            k_to = kept.at[t * BLOCK : (t + 1) * BLOCK]
            v_to = kept.at[seen + t * BLOCK : seen + (t + 1) * BLOCK]
            pltpu.make_async_copy(came[0].at[:BLOCK], k_to, sems.at[2 * t]).wait()
            pltpu.make_async_copy(came[0].at[BLOCK:], v_to, sems.at[2 * t + 1]).wait()

    def work(early, late, early_out, late_out):
        for j in range(per):
            col = slice(j * HD, (j + 1) * HD)
            cache = pl.ds(pl.multiple_of((h * per + j) * HD, HD), HD)
            first = [kept[:seen, cache], early[0][1][:, col], early[1][1][:, col]]
            k = jnp.concatenate(first + [late[0][1][:, col], late[1][1][:, col]], axis=0)
            first = [kept[seen:, cache], early[0][2][:, col], early[1][2][:, col]]
            v = jnp.concatenate(first + [late[0][2][:, col], late[1][2][:, col]], axis=0)
            span = seen + 2 * rows
            q = jnp.concatenate([early[0][0][:, col], early[1][0][:, col]], axis=0)
            scores = logits(q, k[:span], factor)
            mixed = soft(scores + near[...], v[:span])
            early_out[0][:, col] = mixed[:rows]
            early_out[1][:, col] = mixed[rows:]
            q = jnp.concatenate([late[0][0][:, col], late[1][0][:, col]], axis=0)
            mixed = soft(logits(q, k, factor) + bias[...], v)
            late_out[0][:, col] = mixed[:rows]
            late_out[1][:, col] = mixed[rows:]

    @pl.when(at_ref[2] == 0)
    def _():
        work((own, sub), (head, diag), outs[:2], outs[2:])

    @pl.when(at_ref[2] == 1)
    def _():
        work((head, diag), (own, sub), outs[2:], outs[:2])


def assemble_kernel(n, width, chunks, at_ref, *refs):
    arrays, result, sems = refs[:-2], refs[-2], refs[-1]
    pairs = []
    for i, (start, size) in enumerate(chunks):
        for d in range(n):
            to = (at_ref[0] ^ d) * width + start
            to = pl.ds(pl.multiple_of(to, HD), size)
            pairs.append((arrays[i * n + d], result.at[:, to]))
    run_copies(pairs, sems)


def pipelined(n_seq, chunk_heads, queries, new_keys, new_values, key_cache, value_cache, selection):
    n = 4
    rows, features = queries.shape
    width = features // n
    heads = width // HD
    chunks, first = [], 0
    for count in chunk_heads(heads):
        chunks.append((first * HD, count * HD))
        first += count
    r, c = lax.axis_index("head"), lax.axis_index("sub")
    at = jnp.stack([2 * r + c, lax.axis_index("seq"), r, c]).astype(jnp.int32)
    factor = float(HD) ** (-0.5) * LOG2E
    blk_dev = key_cache.shape[0] // BLOCK
    anywhere = pl.BlockSpec(memory_space=pl.ANY)
    bf16 = jnp.bfloat16

    def copier(kernel, name, scalars, arrays, shapes, copies):
        return pl.pallas_call(
            kernel,
            out_shape=[jax.ShapeDtypeStruct(s, bf16) for s in shapes],
            grid_spec=pltpu.PrefetchScalarGridSpec(
                num_scalar_prefetch=len(scalars),
                grid=(1,),
                in_specs=[anywhere] * len(arrays),
                out_specs=[pl.BlockSpec(s, lambda *_: (0, 0)) for s in shapes],
                scratch_shapes=[pltpu.SemaphoreType.DMA((copies,))],
            ),
            name=name,
        )(*scalars, *arrays)

    def exchange(name, d, x):
        with jax.named_scope(name):
            return lax.ppermute(x, ("head", "sub"), [(i, i ^ d) for i in range(n)])

    def along(name, d, x):
        with jax.named_scope(name):
            return lax.ppermute(x, "seq", [(i, i ^ d) for i in range(n_seq)])

    def pack(i, after):
        start, size = chunks[i]
        return copier(
            functools.partial(pack_kernel, n, width, start, size), f"pack{i}", [at],
            [queries, new_keys, new_values, after], [(rows, 3 * size)] * (n - 1), 3 * (n - 1),
        )

    packed = [pack(0, queries)]
    sends = copier(
        functools.partial(sends_kernel, n_seq, blk_dev, chunks), "sends", [at, selection],
        [key_cache, value_cache, packed[0][0]],
        [(2 * BLOCK, size) for _, size in chunks for _ in range(n_seq - 1)],
        2 * (n_seq - 1) * len(chunks),
    )
    for i in range(1, len(chunks)):
        packed.append(pack(i, sends[0]))

    def attend(i, given, came):
        start, size = chunks[i]
        count = size // HD
        per = 2 if count % 2 == 0 else 1
        cols = per * HD
        steps, blocks, base = count // per, width // cols, start // cols

        def own_spec():
            return pl.BlockSpec((rows, cols), lambda h, a, s: (0, a[0] * blocks + base + h))

        def piece(t):
            return pl.BlockSpec((rows, cols), lambda h, a, s: (0, t * steps + h))

        topk = selection.shape[1]
        span = topk * BLOCK + 4 * rows
        return pl.pallas_call(
            functools.partial(attend_kernel, per, n_seq, blk_dev, start, size, factor),
            out_shape=[jax.ShapeDtypeStruct((rows, size), bf16)] * n,
            grid_spec=pltpu.PrefetchScalarGridSpec(
                num_scalar_prefetch=2,
                grid=(steps,),
                in_specs=[own_spec() for _ in range(3)]
                + [piece(t) for _ in range(n - 1) for t in range(3)]
                + [anywhere] * (2 + n_seq - 1),
                out_specs=[pl.BlockSpec((rows, cols), lambda h, a, s: (0, h))] * n,
                scratch_shapes=[
                    pltpu.VMEM((2 * topk * BLOCK, size), bf16),
                    pltpu.VMEM((2 * rows, span - 2 * rows), jnp.float32),
                    pltpu.VMEM((2 * rows, span), jnp.float32),
                    pltpu.SemaphoreType.DMA((2 * topk,)),
                ],
            ),
            name=f"attend{i}",
        )(
            at, selection, queries, new_keys, new_values,
            *[x for x in given for _ in range(3)], key_cache, value_cache, *came,
        )

    pieces = []
    for i in range(len(chunks)):
        given = [exchange(f"qkv{i}_{d}", d, packed[i][d - 1]) for d in range(1, n)]
        came = [
            along(f"cache{i}_{d}", d, sends[i * (n_seq - 1) + d - 1]) for d in range(1, n_seq)
        ]
        outs = attend(i, given, came)
        pieces.append(outs[0])
        pieces += [exchange(f"out{i}_{d}", d, outs[d]) for d in range(1, n)]
    return copier(
        functools.partial(assemble_kernel, n, width, chunks), "assemble", [at],
        pieces, [(rows, features)], n * len(chunks),
    )[0]


def halves(heads):
    return (heads - heads // 2, heads // 2)


def solution(mesh):
    subs = mesh.shape["sub"]
    n = mesh.shape["head"] * subs
    placed = (
        P(("groups", "seq", "head", "sub"), None),
        P(("groups", "seq", "head", "sub"), None),
        P(("groups", "seq", "head", "sub"), None),
        P(("groups", "seq"), ("head", "sub")),
        P(("groups", "seq"), ("head", "sub")),
        P("groups", None),
    )
    n_seq = mesh.shape["seq"]
    body = functools.partial(ulysses, n, subs)
    if (mesh.shape["head"], subs, n_seq) == (2, 2, 4):
        body = functools.partial(pipelined, n_seq, halves)
    return jax.shard_map(
        body,
        mesh=mesh,
        in_specs=placed,
        out_specs=P(("groups", "seq", "head", "sub"), None),
        check_vma=False,
    )
```

```python
import functools

import jax
import jax.numpy as jnp
from jax import lax
from jax.experimental import pallas as pl
from jax.experimental.pallas import tpu as pltpu
from jax.sharding import PartitionSpec as P


HD = 128
BLOCK = 64
LOG2E = 1.4426950408889634
MASKED = -1e30
VMEM_LIMIT = 16 << 20


def softmax_rows(scores, values):
    top = functools.reduce(jnp.maximum, [jnp.max(s, axis=1, keepdims=True) for s in scores])
    weights = [jnp.exp2(s - top) for s in scores]
    total = functools.reduce(jnp.add, [jnp.sum(w, axis=1, keepdims=True) for w in weights])
    mixed = functools.reduce(
        jnp.add,
        [
            jnp.dot(w.astype(jnp.bfloat16), v, preferred_element_type=jnp.float32)
            for w, v in zip(weights, values)
        ],
    )
    return mixed, top, total


def logits(q, k, factor):
    return lax.dot_general(
        q, k, (((1,), (1,)), ((), ())), preferred_element_type=jnp.float32
    ) * factor


def ulysses_kernel(n, topk, per, parts, factor, where_ref, own_ref, *refs):
    qs, ks, vs = refs[:n], refs[n : 2 * n], refs[2 * n : 3 * n]
    cks, cvs = refs[3 * n : 3 * n + topk], refs[3 * n + topk : 3 * n + 2 * topk]
    out_ref, q_all, k_all, v_all = refs[3 * n + 2 * topk :]
    rows = qs[0].shape[0]
    count = rows * n
    for b in range(n):
        at = pl.ds(pl.multiple_of(where_ref[1 + b] * rows, rows), rows)
        q_all[at, :] = qs[b][...]
        k_all[at, :] = ks[b][...]
        v_all[at, :] = vs[b][...]
    step = count // parts
    causal = lax.broadcasted_iota(jnp.int32, (step, step), 0) >= lax.broadcasted_iota(
        jnp.int32, (step, step), 1
    )
    for j in range(per):
        col = slice(j * HD, (j + 1) * HD)
        ck = [r[0, :, col] for r in cks]
        cv = [r[0, :, col] for r in cvs]
        ck = jnp.concatenate(ck, axis=0)
        cv = jnp.concatenate(cv, axis=0)
        for i in range(parts):
            here = slice(i * step, (i + 1) * step)
            q = q_all[here, col]
            scores = [logits(q, ck, factor)]
            values = [cv]
            if i > 0:
                scores.append(logits(q, k_all[: i * step, col], factor))
                values.append(v_all[: i * step, col])
            scores.append(jnp.where(causal, logits(q, k_all[here, col], factor), MASKED))
            values.append(v_all[here, col])
            mixed, _, total = softmax_rows(scores, values)
            out_ref[here, col] = (mixed / total).astype(jnp.bfloat16)


def ulysses(n, subs, queries, new_keys, new_values, key_cache, value_cache, selection):
    rows, features = queries.shape
    width = features // n
    heads = width // HD
    topk = selection.shape[1]
    me = lax.axis_index("seq")
    group = lax.axis_index("head") * subs + lax.axis_index("sub")

    def peer(b):
        return lax.rem(group + b, n)

    def exchange(b, piece):
        return lax.ppermute(piece, ("head", "sub"), [(i, (i + b) % n) for i in range(n)])

    def spread(array):
        pieces = [array]
        for b in range(1, n):
            piece = lax.dynamic_slice_in_dim(array, peer(b) * width, width, axis=1)
            pieces.append(exchange(b, piece))
        return pieces

    blk_dev = key_cache.shape[0] // BLOCK
    owner_of = selection // blk_dev
    inner = jnp.sum(jnp.where(owner_of == me, selection % blk_dev, 0), axis=1)
    mine = lax.dynamic_index_in_dim(selection, me, 0, keepdims=False) // blk_dev
    got = [
        lax.all_to_all(
            cache.reshape(blk_dev, BLOCK, -1)[inner], "seq", split_axis=0, concat_axis=0, tiled=True
        )
        for cache in (key_cache, value_cache)
    ]
    q_pieces, k_pieces, v_pieces = spread(queries), spread(new_keys), spread(new_values)
    from_of = jnp.stack([group] + [lax.rem(group + b, n) for b in range(n, 0, -1)]).astype(jnp.int32)
    per = 2 if heads % 2 == 0 else 1
    cols = per * HD
    own = pl.BlockSpec((rows, cols), lambda h, w, o: (0, w[0] * (heads // per) + h))
    other = pl.BlockSpec((rows, cols), lambda h, w, o: (0, h))
    cached = [
        pl.BlockSpec((1, BLOCK, cols), functools.partial(lambda t, h, w, o: (o[t], 0, h), t))
        for t in range(topk)
    ]
    count = rows * n
    out = pl.pallas_call(
        functools.partial(
            ulysses_kernel, n, topk, per, 2, float(HD) ** (-0.5) * LOG2E
        ),
        out_shape=jax.ShapeDtypeStruct((count, width), jnp.bfloat16),
        grid_spec=pltpu.PrefetchScalarGridSpec(
            num_scalar_prefetch=2,
            grid=(heads // per,),
            in_specs=([own] + [other] * (n - 1)) * 3 + cached * 2,
            out_specs=pl.BlockSpec((count, cols), lambda h, w, o: (0, h)),
            scratch_shapes=[pltpu.VMEM((count, cols), jnp.bfloat16)] * 3,
        ),
        name="attend",
    )(from_of, mine, *q_pieces, *k_pieces, *v_pieces, *([got[0]] * topk), *([got[1]] * topk))
    result = jnp.zeros((rows, features), jnp.bfloat16)
    for b in range(n):
        piece = lax.dynamic_slice_in_dim(out, peer(b) * rows, rows, axis=0)
        if b > 0:
            piece = exchange(b, piece)
        result = lax.dynamic_update_slice_in_dim(
            result, piece, lax.rem(group + n - b, n) * width, axis=1
        )
    return result


def chip_bias(bias, place, rows):
    def token(at):
        return jnp.where(at < rows, place * rows + at, (1 - place) * rows + at - rows)

    q = token(lax.broadcasted_iota(jnp.int32, bias.shape, 0))
    k = lax.broadcasted_iota(jnp.int32, bias.shape, 1)
    bias[...] = jnp.where((k >= 2 * rows) | (q >= token(k)), 0.0, MASKED)


def soft(scores, values):
    top = jnp.max(scores, axis=1, keepdims=True)
    weights = jnp.exp2(scores - top)
    total = jnp.sum(weights, axis=1, keepdims=True)
    mixed = jnp.dot(weights.astype(jnp.bfloat16), values, preferred_element_type=jnp.float32)
    return (mixed * (1.0 / total)).astype(jnp.bfloat16)


def group_index():
    return lax.axis_index("head") * 2 + lax.axis_index("sub")


def run_copies(pairs, sems):
    copies = [pltpu.make_async_copy(a, b, sems.at[i]) for i, (a, b) in enumerate(pairs)]
    for copy in copies:
        copy.start()
    for copy in copies:
        copy.wait()


def held(sel_ref, row, owner, blk_dev):
    inner = jnp.int32(0)
    for t in range(sel_ref.shape[0]):
        picked = sel_ref[t, row]
        match = lax.div(picked, jnp.int32(blk_dev)) == owner
        inner = jnp.where(match, lax.rem(picked, jnp.int32(blk_dev)), inner)
    return inner


def pack_kernel(width, wanted, q, k, v, after, *refs):
    outs, sems = refs[:-1], refs[-1]
    pairs = []
    for out, (d, start, size) in zip(outs, wanted):
        at = (group_index() ^ d) * width + start
        cols = pl.ds(pl.multiple_of(at, HD), size)
        for i, array in enumerate((q, k, v)):
            pairs.append((array.at[:, cols], out.at[:, i * size : (i + 1) * size]))
    run_copies(pairs, sems)


def sends_kernel(n_seq, blk_dev, rows, chunks, sel_ref, kc, vc, after, *refs):
    outs, bias, sems = refs[:-2], refs[-2], refs[-1]
    me = lax.axis_index("seq")
    pairs = []
    for i, (start, size) in enumerate(chunks):
        for d in range(n_seq):
            inner = held(sel_ref, me ^ d, me, blk_dev)
            at = pl.ds(pl.multiple_of(inner * BLOCK, BLOCK), BLOCK)
            to = outs[i * n_seq + d]
            pairs.append((kc.at[at, start : start + size], to.at[:BLOCK]))
            pairs.append((vc.at[at, start : start + size], to.at[BLOCK:]))
    copies = [pltpu.make_async_copy(a, b, sems.at[i]) for i, (a, b) in enumerate(pairs)]
    for copy in copies:
        copy.start()
    chip_bias(bias, lax.axis_index("sub"), rows)
    for copy in copies:
        copy.wait()


def attend_kernel(n, n_seq, per, blk_dev, size, factor, sel_ref, bias, *refs):
    given, came = refs[:n], refs[n : n + n_seq]
    outs, kept = refs[n + n_seq : 2 * n + n_seq], refs[2 * n + n_seq]
    rows = given[0].shape[0]
    topk = sel_ref.shape[0]
    seen = topk * BLOCK
    me = lax.axis_index("seq")
    for t in range(topk):
        distance = lax.div(sel_ref[t, me], jnp.int32(blk_dev)) ^ me
        for d in range(n_seq):

            @pl.when(distance == d)
            def _():
                kept[t * BLOCK : (t + 1) * BLOCK] = came[d][:BLOCK]
                kept[seen + t * BLOCK : seen + (t + 1) * BLOCK] = came[d][BLOCK:]

    def work(early, late):
        def step(h, carry):
            for j in range(per):
                head = (h * per + j) * HD
                col = pl.ds(pl.multiple_of(head, HD), HD)

                def pick(side, t):
                    at = pl.ds(pl.multiple_of(t * size + head, HD), HD)
                    return [given[d][:, at] for d in side]

                kept_k, kept_v = kept[:seen, col], kept[seen:, col]
                early_k, early_v = pick(early, 1), pick(early, 2)
                for side, k, v in (
                    (early, early_k, early_v),
                    (late, pick(late, 1) + early_k, pick(late, 2) + early_v),
                ):
                    q = jnp.concatenate(pick(side, 0), axis=0)
                    scores = logits(q, jnp.concatenate([kept_k] + k, axis=0), factor)
                    masked = min(bias.shape[1], scores.shape[1] - seen)
                    parts = [scores[:, :seen], scores[:, seen : seen + masked] + bias[:, :masked]]
                    if scores.shape[1] > seen + masked:
                        parts.append(scores[:, seen + masked :])
                    mixed = soft(
                        jnp.concatenate(parts, axis=1), jnp.concatenate([kept_v] + v, axis=0)
                    )
                    outs[side[0]][:, col] = mixed[:rows]
                    outs[side[1]][:, col] = mixed[rows:]
            return carry

        lax.fori_loop(0, size // HD // per, step, 0)

    @pl.when(lax.axis_index("head") == 0)
    def _():
        work((0, 1), (2, 3))

    @pl.when(lax.axis_index("head") == 1)
    def _():
        work((2, 3), (0, 1))


def assemble_kernel(n, width, start, size, count, *refs):
    arrays, result, sems = refs[:n], refs[count], refs[-1]
    pairs = []
    for d in range(n):
        to = (group_index() ^ d) * width + start
        pairs.append((arrays[d], result.at[:, pl.ds(pl.multiple_of(to, HD), size)]))
    run_copies(pairs, sems)


def pipelined(n_seq, chunk_heads, queries, new_keys, new_values, key_cache, value_cache, selection):
    n = 4
    rows, features = queries.shape
    width = features // n
    heads = width // HD
    chunks, first = [], 0
    for count in chunk_heads(heads):
        chunks.append((first * HD, count * HD))
        first += count
    factor = float(HD) ** (-0.5) * LOG2E
    blk_dev = key_cache.shape[0] // BLOCK
    anywhere = pl.BlockSpec(memory_space=pl.ANY)
    resident = pl.BlockSpec(memory_space=pltpu.VMEM)
    bf16 = jnp.bfloat16

    def call(kernel, scalars, arrays, in_specs, outs, scratch):
        return pl.pallas_call(
            kernel,
            out_shape=[
                jax.ShapeDtypeStruct(*o) if isinstance(o, tuple) else o for o in outs
            ],
            grid_spec=pltpu.PrefetchScalarGridSpec(
                num_scalar_prefetch=len(scalars),
                grid=(1,),
                in_specs=in_specs,
                out_specs=[
                    pl.BlockSpec(o[0], lambda *_: (0, 0)) if isinstance(o, tuple) else resident
                    for o in outs
                ],
                scratch_shapes=scratch,
            ),
            compiler_params=pltpu.CompilerParams(vmem_limit_bytes=VMEM_LIMIT),
        )(*scalars, *arrays)

    def exchange(d, x):
        return lax.ppermute(x, ("head", "sub"), [(i, i ^ d) for i in range(n)])

    def along(d, x):
        return lax.ppermute(x, "seq", [(i, i ^ d) for i in range(n_seq)])

    def pack(wanted, after):
        return call(
            functools.partial(pack_kernel, width, wanted), [],
            [queries, new_keys, new_values, after], [anywhere] * 4,
            [pltpu.VMEM((rows, 3 * size), bf16) for _, _, size in wanted],
            [pltpu.SemaphoreType.DMA((3 * len(wanted),))],
        )

    last = len(chunks) - 1
    picks = selection.T
    packed = [pack([(d, *chunks[0]) for d in range(1, n)], queries)]
    sends = call(
        functools.partial(sends_kernel, n_seq, blk_dev, rows, chunks), [picks],
        [key_cache, value_cache, packed[0][0]], [anywhere] * 3,
        [
            pltpu.VMEM((2 * BLOCK, size), bf16)
            for _, size in chunks
            for _ in range(n_seq)
        ]
        + [pltpu.VMEM((2 * rows, pl.cdiv(2 * rows, HD) * HD), jnp.float32)],
        [pltpu.SemaphoreType.DMA((2 * n_seq * len(chunks),))],
    )
    bias = sends[-1]
    for i in range(1, len(chunks)):
        packed.append(pack([(d, *chunks[i]) for d in range(1, n)], sends[1]))
    owned = pack([(0, *chunk) for chunk in chunks], packed[last][0])

    def attend(i, given, came):
        size = chunks[i][1]
        count = size // HD
        return call(
            functools.partial(
                attend_kernel, n, n_seq, 2 if count % 2 == 0 else 1, blk_dev, size, factor
            ),
            [picks], [bias, *given, *came], [resident] * (1 + n + n_seq),
            [pltpu.VMEM((rows, size), bf16)] * n,
            [pltpu.VMEM((2 * selection.shape[1] * BLOCK, size), bf16)],
        )

    result = None
    for i, (start, size) in enumerate(chunks):
        given = [exchange(d, packed[i][d - 1]) for d in range(1, n)]
        given = [owned[i]] + given
        block = sends[i * n_seq : (i + 1) * n_seq]
        came = [block[0]] + [along(d, block[d]) for d in range(1, n_seq)]
        outs = attend(i, given, came)
        pieces = [outs[0]] + [exchange(d, outs[d]) for d in range(1, n)]
        if result is not None:
            pieces.append(result)
        result = pl.pallas_call(
            functools.partial(assemble_kernel, n, width, start, size, len(pieces)),
            out_shape=jax.ShapeDtypeStruct((rows, features), bf16),
            grid_spec=pltpu.PrefetchScalarGridSpec(
                num_scalar_prefetch=0,
                grid=(1,),
                in_specs=[resident] * n + [anywhere] * (len(pieces) - n),
                out_specs=anywhere,
                scratch_shapes=[pltpu.SemaphoreType.DMA((n,))],
            ),
            input_output_aliases={n: 0} if i > 0 else {},
            compiler_params=pltpu.CompilerParams(vmem_limit_bytes=VMEM_LIMIT),
        )(*pieces)
    return result


def uneven(heads):
    second = max(2, heads * 3 // 8 // 2 * 2)
    return (heads - second, second)


def placed_map(body, mesh, placed):
    return jax.shard_map(
        body,
        mesh=mesh,
        in_specs=placed,
        out_specs=P(("groups", "seq", "head", "sub"), None),
        check_vma=False,
    )


def solution(mesh):
    subs = mesh.shape["sub"]
    n = mesh.shape["head"] * subs
    placed = (
        P(("groups", "seq", "head", "sub"), None),
        P(("groups", "seq", "head", "sub"), None),
        P(("groups", "seq", "head", "sub"), None),
        P(("groups", "seq"), ("head", "sub")),
        P(("groups", "seq"), ("head", "sub")),
        P("groups", None),
    )
    n_seq = mesh.shape["seq"]
    body = functools.partial(ulysses, n, subs)
    if (mesh.shape["head"], subs, n_seq) == (2, 2, 4):
        body = functools.partial(pipelined, n_seq, uneven)
    if (mesh.shape["head"], subs, n_seq) != (2, 2, 4):
        return placed_map(body, mesh, placed)

    def step(*args):
        return body(*args)

    return placed_map(step, mesh, placed)
```

```python
import functools

import jax
import jax.numpy as jnp
from jax import lax
from jax.experimental import pallas as pl
from jax.experimental.pallas import tpu as pltpu
from jax.sharding import PartitionSpec as P


HD = 128
BLOCK = 64
LOG2E = 1.4426950408889634
MASKED = -1e30
VMEM_LIMIT = 16 << 20


def softmax_rows(scores, values):
    top = functools.reduce(jnp.maximum, [jnp.max(s, axis=1, keepdims=True) for s in scores])
    weights = [jnp.exp2(s - top) for s in scores]
    total = functools.reduce(jnp.add, [jnp.sum(w, axis=1, keepdims=True) for w in weights])
    mixed = functools.reduce(
        jnp.add,
        [
            jnp.dot(w.astype(jnp.bfloat16), v, preferred_element_type=jnp.float32)
            for w, v in zip(weights, values)
        ],
    )
    return mixed, top, total


def logits(q, k, factor):
    return lax.dot_general(
        q, k, (((1,), (1,)), ((), ())), preferred_element_type=jnp.float32
    ) * factor


def ulysses_kernel(n, topk, per, parts, factor, where_ref, own_ref, *refs):
    qs, ks, vs = refs[:n], refs[n : 2 * n], refs[2 * n : 3 * n]
    cks, cvs = refs[3 * n : 3 * n + topk], refs[3 * n + topk : 3 * n + 2 * topk]
    out_ref, q_all, k_all, v_all = refs[3 * n + 2 * topk :]
    rows = qs[0].shape[0]
    count = rows * n
    for b in range(n):
        at = pl.ds(pl.multiple_of(where_ref[1 + b] * rows, rows), rows)
        q_all[at, :] = qs[b][...]
        k_all[at, :] = ks[b][...]
        v_all[at, :] = vs[b][...]
    step = count // parts
    causal = lax.broadcasted_iota(jnp.int32, (step, step), 0) >= lax.broadcasted_iota(
        jnp.int32, (step, step), 1
    )
    for j in range(per):
        col = slice(j * HD, (j + 1) * HD)
        ck = [r[0, :, col] for r in cks]
        cv = [r[0, :, col] for r in cvs]
        ck = jnp.concatenate(ck, axis=0)
        cv = jnp.concatenate(cv, axis=0)
        for i in range(parts):
            here = slice(i * step, (i + 1) * step)
            q = q_all[here, col]
            scores = [logits(q, ck, factor)]
            values = [cv]
            if i > 0:
                scores.append(logits(q, k_all[: i * step, col], factor))
                values.append(v_all[: i * step, col])
            scores.append(jnp.where(causal, logits(q, k_all[here, col], factor), MASKED))
            values.append(v_all[here, col])
            mixed, _, total = softmax_rows(scores, values)
            out_ref[here, col] = (mixed / total).astype(jnp.bfloat16)


def ulysses(n, subs, queries, new_keys, new_values, key_cache, value_cache, selection):
    rows, features = queries.shape
    width = features // n
    heads = width // HD
    topk = selection.shape[1]
    me = lax.axis_index("seq")
    group = lax.axis_index("head") * subs + lax.axis_index("sub")

    def peer(b):
        return lax.rem(group + b, n)

    def exchange(b, piece):
        return lax.ppermute(piece, ("head", "sub"), [(i, (i + b) % n) for i in range(n)])

    def spread(array):
        pieces = [array]
        for b in range(1, n):
            piece = lax.dynamic_slice_in_dim(array, peer(b) * width, width, axis=1)
            pieces.append(exchange(b, piece))
        return pieces

    blk_dev = key_cache.shape[0] // BLOCK
    owner_of = selection // blk_dev
    inner = jnp.sum(jnp.where(owner_of == me, selection % blk_dev, 0), axis=1)
    mine = lax.dynamic_index_in_dim(selection, me, 0, keepdims=False) // blk_dev
    got = [
        lax.all_to_all(
            cache.reshape(blk_dev, BLOCK, -1)[inner], "seq", split_axis=0, concat_axis=0, tiled=True
        )
        for cache in (key_cache, value_cache)
    ]
    q_pieces, k_pieces, v_pieces = spread(queries), spread(new_keys), spread(new_values)
    from_of = jnp.stack([group] + [lax.rem(group + b, n) for b in range(n, 0, -1)]).astype(jnp.int32)
    per = 2 if heads % 2 == 0 else 1
    cols = per * HD
    own = pl.BlockSpec((rows, cols), lambda h, w, o: (0, w[0] * (heads // per) + h))
    other = pl.BlockSpec((rows, cols), lambda h, w, o: (0, h))
    cached = [
        pl.BlockSpec((1, BLOCK, cols), functools.partial(lambda t, h, w, o: (o[t], 0, h), t))
        for t in range(topk)
    ]
    count = rows * n
    out = pl.pallas_call(
        functools.partial(
            ulysses_kernel, n, topk, per, 2, float(HD) ** (-0.5) * LOG2E
        ),
        out_shape=jax.ShapeDtypeStruct((count, width), jnp.bfloat16),
        grid_spec=pltpu.PrefetchScalarGridSpec(
            num_scalar_prefetch=2,
            grid=(heads // per,),
            in_specs=([own] + [other] * (n - 1)) * 3 + cached * 2,
            out_specs=pl.BlockSpec((count, cols), lambda h, w, o: (0, h)),
            scratch_shapes=[pltpu.VMEM((count, cols), jnp.bfloat16)] * 3,
        ),
        name="attend",
    )(from_of, mine, *q_pieces, *k_pieces, *v_pieces, *([got[0]] * topk), *([got[1]] * topk))
    result = jnp.zeros((rows, features), jnp.bfloat16)
    for b in range(n):
        piece = lax.dynamic_slice_in_dim(out, peer(b) * rows, rows, axis=0)
        if b > 0:
            piece = exchange(b, piece)
        result = lax.dynamic_update_slice_in_dim(
            result, piece, lax.rem(group + n - b, n) * width, axis=1
        )
    return result


def chip_bias(bias, place, rows):
    def token(at):
        return jnp.where(at < rows, place * rows + at, (1 - place) * rows + at - rows)

    q = token(lax.broadcasted_iota(jnp.int32, bias.shape, 0))
    k = lax.broadcasted_iota(jnp.int32, bias.shape, 1)
    bias[...] = jnp.where((k >= 2 * rows) | (q >= token(k)), 0.0, MASKED)


def biased(scores, seen, bias):
    masked = min(bias.shape[1], scores.shape[1] - seen)
    parts = [scores[:, seen : seen + masked] + bias[:, :masked]]
    if seen > 0:
        parts.insert(0, scores[:, :seen])
    if scores.shape[1] > seen + masked:
        parts.append(scores[:, seen + masked :])
    return jnp.concatenate(parts, axis=1)


def soft(scores, values):
    top = jnp.max(scores, axis=1, keepdims=True)
    weights = jnp.exp2(scores - top)
    total = jnp.sum(weights, axis=1, keepdims=True)
    mixed = jnp.dot(weights.astype(jnp.bfloat16), values, preferred_element_type=jnp.float32)
    return mixed, top, total


def held(sel_ref, row, owner, blk_dev):
    inner = jnp.int32(0)
    for t in range(sel_ref.shape[0]):
        picked = sel_ref[t, row]
        match = lax.div(picked, jnp.int32(blk_dev)) == owner
        inner = jnp.where(match, lax.rem(picked, jnp.int32(blk_dev)), inner)
    return inner


def group_index():
    return lax.axis_index("head") * 2 + lax.axis_index("sub")


def run_copies(pairs, sems):
    copies = [pltpu.make_async_copy(a, b, sems.at[i]) for i, (a, b) in enumerate(pairs)]
    for copy in copies:
        copy.start()
    for copy in copies:
        copy.wait()


def cross_kernel(width, start, size, q, k, v, after, two, three, sems):
    def pairs(arrays):
        result = []
        for out, d in ((two, 2), (three, 3)):
            at = (group_index() ^ d) * width + start
            cols = pl.ds(pl.multiple_of(at, HD), size)
            for i, array in enumerate(arrays):
                result.append((array.at[:, cols], out.at[:, i * size : (i + 1) * size]))
        return result

    @pl.when(lax.axis_index("head") == 0)
    def _():
        run_copies(pairs((k, v)), sems)

    @pl.when(lax.axis_index("head") == 1)
    def _():
        run_copies(pairs((q, q)), sems)


def core_kernel(width, start, size, flip, q, k, v, after, out, sems):
    pairs = []
    for i in range(2):
        at = (2 * i + (lax.axis_index("sub") ^ flip)) * width + start
        cols = pl.ds(pl.multiple_of(at, HD), size)
        for t, array in enumerate((q, k, v)):
            to = (3 * i + t) * size
            pairs.append((array.at[:, cols], out.at[:, to : to + size]))
    run_copies(pairs, sems)


def sends_kernel(n_seq, blk_dev, rows, chunks, sel_ref, kc, vc, *refs):
    outs, bias, sems = refs[:-2], refs[-2], refs[-1]
    me = lax.axis_index("seq")
    pairs = []
    for i, (start, size) in enumerate(chunks):
        for d in range(n_seq):
            inner = held(sel_ref, me ^ d, me, blk_dev)
            at = pl.ds(pl.multiple_of(inner * BLOCK, BLOCK), BLOCK)
            to = outs[i * n_seq + d]
            pairs.append((kc.at[at, start : start + size], to.at[:BLOCK]))
            pairs.append((vc.at[at, start : start + size], to.at[BLOCK:]))
    copies = [pltpu.make_async_copy(a, b, sems.at[i]) for i, (a, b) in enumerate(pairs)]
    for copy in copies:
        copy.start()
    chip_bias(bias, lax.axis_index("sub"), rows)
    for copy in copies:
        copy.wait()


def collect_kernel(blk_dev, sel_ref, *refs):
    sources, kept = refs[:-1], refs[-1]
    me = lax.axis_index("seq")
    topk = sel_ref.shape[0]
    for t in range(topk):
        distance = lax.div(sel_ref[t, me], jnp.int32(blk_dev)) ^ me
        for d, source in enumerate(sources):

            @pl.when(distance == d)
            def _():
                kept[t * BLOCK : (t + 1) * BLOCK] = source[:BLOCK]
                kept[(topk + t) * BLOCK : (topk + t + 1) * BLOCK] = source[BLOCK:]


def lane_put(into, lane, column):
    lanes = lax.broadcasted_iota(jnp.int32, into.shape, 1)
    return jnp.where(lanes == lane, column, into)


def early_kernel(per, size, factor, bias, own, par, two, three, kept, loc0, loc1, part0, part1):
    rows = own.shape[0]
    heads = size // HD
    locs, parts = (loc0, loc1), (part0, part1)
    for loc in locs:
        loc[:, size:] = jnp.zeros((rows, HD), jnp.float32)

    def columns(h, j):
        head = (h * per + j) * HD

        def pick(t):
            at = pl.ds(pl.multiple_of(t * size + head, HD), HD)
            return jnp.concatenate([own[:, at], par[:, at]], axis=0)

        return pl.ds(pl.multiple_of(head, HD), HD), pick

    def put(lane, top, total):
        for i, loc in enumerate(locs):
            at = slice(i * rows, (i + 1) * rows)
            stat = lane_put(loc[:, size:], lane, top[at])
            loc[:, size:] = lane_put(stat, lane + 1, total[at])

    def first_chip(h, carry):
        for j in range(per):
            col, pick = columns(h, j)
            k = jnp.concatenate([kept[: 2 * BLOCK, col], pick(1)], axis=0)
            v = jnp.concatenate([kept[2 * BLOCK :, col], pick(2)], axis=0)
            mixed, top, total = soft(biased(logits(pick(0), k, factor), 2 * BLOCK, bias), v)
            mixed = mixed * (1.0 / total)
            loc0[:, col], loc1[:, col] = mixed[:rows], mixed[rows:]
            q = jnp.concatenate([two[:, col], three[:, col]], axis=0)
            mixed, top, total = soft(logits(q, k, factor), v)
            mixed = (mixed * (1.0 / total)).astype(jnp.bfloat16)
            part0[:, col], part1[:, col] = mixed[:rows], mixed[rows:]
            put((h * per + j) * 2, top, total)
        return carry

    def second_chip(h, carry):
        for j in range(per):
            col, pick = columns(h, j)
            mixed, top, total = soft(biased(logits(pick(0), pick(1), factor), 0, bias), pick(2))
            loc0[:, col], loc1[:, col] = mixed[:rows], mixed[rows:]
            put((h * per + j) * 2, top, total)
        return carry

    @pl.when(lax.axis_index("head") == 0)
    def _():
        lax.fori_loop(0, heads // per, first_chip, 0)
        for loc, part in zip(locs, parts):
            left = loc[:, size:]
            packed = jnp.zeros_like(left)
            for t in range(3):
                piece = left.astype(jnp.bfloat16).astype(jnp.float32)
                left = left - piece
                packed = packed + (pltpu.roll(piece, 2 * heads * t, 1) if t > 0 else piece)
            part[:, size:] = packed.astype(jnp.bfloat16)

    @pl.when(lax.axis_index("head") == 1)
    def _():
        lax.fori_loop(0, heads // per, second_chip, 0)


def late_kernel(per, size, factor, bias, own, par, two, three, kept, crossed, out0, out1):
    rows = own.shape[0]

    def run(cache, with_first):
        def step(h, carry):
            for j in range(per):
                head = (h * per + j) * HD
                col = pl.ds(pl.multiple_of(head, HD), HD)

                def pick(t):
                    at = pl.ds(pl.multiple_of((3 + t) * size + head, HD), HD)
                    return [own[:, at], par[:, at]]

                k, v = [cache[: 2 * BLOCK, col]] + pick(1), [cache[2 * BLOCK :, col]] + pick(2)
                if with_first:
                    there = pl.ds(pl.multiple_of(size + head, HD), HD)
                    k += [two[:, col], three[:, col]]
                    v += [two[:, there], three[:, there]]
                scores = logits(
                    jnp.concatenate(pick(0), axis=0), jnp.concatenate(k, axis=0), factor
                )
                mixed, _, total = soft(biased(scores, 2 * BLOCK, bias), jnp.concatenate(v, axis=0))
                mixed = (mixed * (1.0 / total)).astype(jnp.bfloat16)
                out0[:, col], out1[:, col] = mixed[:rows], mixed[rows:]
            return carry

        lax.fori_loop(0, size // HD // per, step, 0)

    @pl.when(lax.axis_index("head") == 0)
    def _():
        run(crossed, False)

    @pl.when(lax.axis_index("head") == 1)
    def _():
        run(kept, True)


def finish_kernel(width, start, size, count, *refs):
    own, got, loc_own, loc_got, far_own, far_got = refs[:6]
    result, merged_own, merged_got, sems = refs[count:]
    heads = size // HD
    c = lax.axis_index("sub")

    def put(array, group, i):
        to = pl.ds(pl.multiple_of(group * width + start, HD), size)
        return pltpu.make_async_copy(array, result.at[:, to], sems.at[i])

    copies = [put(own, 2 + c, 0), put(got, 3 - c, 1)]
    for copy in copies:
        copy.start()
    pairs = ((loc_own, far_own, merged_own), (loc_got, far_got, merged_got))

    @pl.when(lax.axis_index("head") == 0)
    def _():
        for loc, far, merged in pairs:
            merged[...] = loc[:, :size].astype(jnp.bfloat16)

    @pl.when(lax.axis_index("head") == 1)
    def _():
        for loc, far, merged in pairs:
            packed = far[:, size:].astype(jnp.float32)
            there = packed
            for t in range(1, 3):
                there = there + pltpu.roll(packed, HD - 2 * heads * t, 1)
            here = loc[:, size:]
            for i in range(heads):
                col = slice(i * HD, (i + 1) * HD)
                near_top, near_sum = here[:, 2 * i : 2 * i + 1], here[:, 2 * i + 1 : 2 * i + 2]
                far_top, far_sum = there[:, 2 * i : 2 * i + 1], there[:, 2 * i + 1 : 2 * i + 2]
                top = jnp.maximum(near_top, far_top)
                near = jnp.exp2(near_top - top)
                away = far_sum * jnp.exp2(far_top - top)
                scale = 1.0 / (near_sum * near + away)
                mixed = loc[:, col] * (near * scale)
                mixed = mixed + far[:, col].astype(jnp.float32) * (away * scale)
                merged[:, col] = mixed.astype(jnp.bfloat16)

    copies += [put(merged_own, c, 2), put(merged_got, 1 - c, 3)]
    for copy in copies[2:]:
        copy.start()
    for copy in copies:
        copy.wait()


def hybrid(n_seq, chunk_heads, queries, new_keys, new_values, key_cache, value_cache, selection):
    n = 4
    rows, features = queries.shape
    width = features // n
    heads = width // HD
    chunks, first = [], 0
    for count in chunk_heads(heads):
        chunks.append((first * HD, count * HD))
        first += count
    factor = float(HD) ** (-0.5) * LOG2E
    blk_dev = key_cache.shape[0] // BLOCK
    picks = selection.T
    anywhere = pl.BlockSpec(memory_space=pl.ANY)
    in_hbm = pl.BlockSpec(memory_space=pltpu.HBM)
    resident = pl.BlockSpec(memory_space=pltpu.VMEM)
    bf16, f32 = jnp.bfloat16, jnp.float32

    def call(kernel, arrays, in_specs, shapes, scratch=(), scalars=(), result=None):
        return pl.pallas_call(
            kernel,
            out_shape=[pltpu.VMEM(*s) for s in shapes] if result is None else result,
            grid_spec=pltpu.PrefetchScalarGridSpec(
                num_scalar_prefetch=len(scalars),
                grid=(1,),
                in_specs=in_specs,
                out_specs=[resident] * len(shapes) if result is None else anywhere,
                scratch_shapes=list(scratch),
            ),
            input_output_aliases={6: 0} if len(arrays) == 7 and result is not None else {},
            compiler_params=pltpu.CompilerParams(vmem_limit_bytes=VMEM_LIMIT),
        )(*scalars, *arrays)

    def move(x, pairs, axes=("head", "sub")):
        return lax.ppermute(x, axes, list(pairs))

    def apart(d, sources=range(n)):
        return [(i, i ^ d) for i in sources]

    arrays = [pltpu.with_memory_space_constraint(x, pltpu.HBM) for x in (queries, new_keys, new_values)]
    caches = [pltpu.with_memory_space_constraint(x, pltpu.HBM) for x in (key_cache, value_cache)]
    from_args = [in_hbm] * 3 + [anywhere]

    def cross(i, after):
        start, size = chunks[i]
        sent = call(
            functools.partial(cross_kernel, width, start, size), arrays + [after],
            from_args, [((rows, 2 * size), bf16)] * 2, [pltpu.SemaphoreType.DMA((4,))],
        )
        return sent, [move(sent[d - 2], apart(d)) for d in (2, 3)]

    def cores(i, flip, after):
        start, size = chunks[i]
        return call(
            functools.partial(core_kernel, width, start, size, flip),
            arrays + [after], from_args, [((rows, 6 * size), bf16)],
            [pltpu.SemaphoreType.DMA((6,))],
        )[0]

    sends = call(
        functools.partial(sends_kernel, n_seq, blk_dev, rows, chunks),
        caches, [in_hbm] * 2,
        [((2 * BLOCK, size), bf16) for _, size in chunks for _ in range(n_seq)]
        + [((2 * rows, pl.cdiv(2 * rows, HD) * HD), f32)],
        [pltpu.SemaphoreType.DMA((2 * n_seq * len(chunks),))], [picks],
    )
    bias = sends[-1]
    sent, crossing = [sends[1]], []
    for i in range(len(chunks)):
        sent, came = cross(i, sent[0])
        crossing.append(came)
    own, par, after = [], [], sent[0]
    for i in range(len(chunks)):
        after = cores(i, 1, after)
        par.append(move(after, apart(1)))
    for i in range(len(chunks)):
        after = cores(i, 0, after)
        own.append(after)

    def fetch(i):
        block = sends[n_seq * i : n_seq * (i + 1)]
        came = [block[0]]
        for d in range(1, n_seq):
            came.append(move(block[d], [(z, z ^ d) for z in range(n_seq)], "seq"))
        kept = call(
            functools.partial(collect_kernel, blk_dev), came, [resident] * n_seq,
            [((4 * BLOCK, chunks[i][1]), bf16)], (), [picks],
        )[0]
        return kept, move(kept, apart(2, (2, 3)))

    result = None
    for i, (start, size) in enumerate(chunks):
        kept, crossed = fetch(i)
        per = 2 if size // HD % 2 == 0 else 1
        given = [bias, own[i], par[i], *crossing[i], kept]
        loc0, loc1, part0, part1 = call(
            functools.partial(early_kernel, per, size, factor), given, [resident] * 6,
            [((rows, size + HD), f32)] * 2 + [((rows, size + HD), bf16)] * 2,
        )
        far0 = move(part0, apart(2, (0, 1)))
        far1 = move(part1, apart(3, (0, 1)))
        got_loc = move(loc1, apart(1))
        out0, out1 = call(
            functools.partial(late_kernel, per, size, factor), given + [crossed],
            [resident] * 7, [((rows, size), bf16)] * 2,
        )
        got = move(out1, apart(1))
        pieces = [out0, got, loc0, got_loc, far0, far1]
        specs = [resident] * 6
        if result is not None:
            pieces, specs = pieces + [result], specs + [anywhere]
        result = call(
            functools.partial(finish_kernel, width, start, size, len(pieces)),
            pieces, specs, [],
            [pltpu.VMEM((rows, size), bf16)] * 2 + [pltpu.SemaphoreType.DMA((4,))],
            (), jax.ShapeDtypeStruct((rows, features), bf16),
        )
    return result


def uneven(heads):
    second = max(2, heads * 3 // 8 // 2 * 2)
    return (heads - second, second)


def placed_map(body, mesh, placed):
    return jax.shard_map(
        body,
        mesh=mesh,
        in_specs=placed,
        out_specs=P(("groups", "seq", "head", "sub"), None),
        check_vma=False,
    )


def solution(mesh):
    subs = mesh.shape["sub"]
    n = mesh.shape["head"] * subs
    placed = (
        P(("groups", "seq", "head", "sub"), None),
        P(("groups", "seq", "head", "sub"), None),
        P(("groups", "seq", "head", "sub"), None),
        P(("groups", "seq"), ("head", "sub")),
        P(("groups", "seq"), ("head", "sub")),
        P("groups", None),
    )
    n_seq = mesh.shape["seq"]
    body = functools.partial(ulysses, n, subs)
    if (mesh.shape["head"], subs, n_seq) == (2, 2, 4):
        body = functools.partial(hybrid, n_seq, uneven)
    if (mesh.shape["head"], subs, n_seq) != (2, 2, 4):
        return placed_map(body, mesh, placed)

    def step(*args):
        return body(*args)

    return placed_map(step, mesh, placed)
```

```python
import functools

import jax
import jax.numpy as jnp
from jax import lax
from jax.experimental import pallas as pl
from jax.experimental.pallas import tpu as pltpu
from jax.sharding import PartitionSpec as P


HD = 128
BLOCK = 64
LOG2E = 1.4426950408889634
MASKED = -1e30
VMEM_LIMIT = 16 << 20


def softmax_rows(scores, values):
    top = functools.reduce(jnp.maximum, [jnp.max(s, axis=1, keepdims=True) for s in scores])
    weights = [jnp.exp2(s - top) for s in scores]
    total = functools.reduce(jnp.add, [jnp.sum(w, axis=1, keepdims=True) for w in weights])
    mixed = functools.reduce(
        jnp.add,
        [
            jnp.dot(w.astype(jnp.bfloat16), v, preferred_element_type=jnp.float32)
            for w, v in zip(weights, values)
        ],
    )
    return mixed, top, total


def logits(q, k, factor):
    return lax.dot_general(
        q, k, (((1,), (1,)), ((), ())), preferred_element_type=jnp.float32
    ) * factor


def ulysses_kernel(n, topk, per, parts, factor, where_ref, own_ref, *refs):
    qs, ks, vs = refs[:n], refs[n : 2 * n], refs[2 * n : 3 * n]
    cks, cvs = refs[3 * n : 3 * n + topk], refs[3 * n + topk : 3 * n + 2 * topk]
    out_ref, q_all, k_all, v_all = refs[3 * n + 2 * topk :]
    rows = qs[0].shape[0]
    count = rows * n
    for b in range(n):
        at = pl.ds(pl.multiple_of(where_ref[1 + b] * rows, rows), rows)
        q_all[at, :] = qs[b][...]
        k_all[at, :] = ks[b][...]
        v_all[at, :] = vs[b][...]
    step = count // parts
    causal = lax.broadcasted_iota(jnp.int32, (step, step), 0) >= lax.broadcasted_iota(
        jnp.int32, (step, step), 1
    )
    for j in range(per):
        col = slice(j * HD, (j + 1) * HD)
        ck = [r[0, :, col] for r in cks]
        cv = [r[0, :, col] for r in cvs]
        ck = jnp.concatenate(ck, axis=0)
        cv = jnp.concatenate(cv, axis=0)
        for i in range(parts):
            here = slice(i * step, (i + 1) * step)
            q = q_all[here, col]
            scores = [logits(q, ck, factor)]
            values = [cv]
            if i > 0:
                scores.append(logits(q, k_all[: i * step, col], factor))
                values.append(v_all[: i * step, col])
            scores.append(jnp.where(causal, logits(q, k_all[here, col], factor), MASKED))
            values.append(v_all[here, col])
            mixed, _, total = softmax_rows(scores, values)
            out_ref[here, col] = (mixed / total).astype(jnp.bfloat16)


def ulysses(n, subs, queries, new_keys, new_values, key_cache, value_cache, selection):
    rows, features = queries.shape
    width = features // n
    heads = width // HD
    topk = selection.shape[1]
    me = lax.axis_index("seq")
    group = lax.axis_index("head") * subs + lax.axis_index("sub")

    def peer(b):
        return lax.rem(group + b, n)

    def exchange(b, piece):
        return lax.ppermute(piece, ("head", "sub"), [(i, (i + b) % n) for i in range(n)])

    def spread(array):
        pieces = [array]
        for b in range(1, n):
            piece = lax.dynamic_slice_in_dim(array, peer(b) * width, width, axis=1)
            pieces.append(exchange(b, piece))
        return pieces

    blk_dev = key_cache.shape[0] // BLOCK
    owner_of = selection // blk_dev
    inner = jnp.sum(jnp.where(owner_of == me, selection % blk_dev, 0), axis=1)
    mine = lax.dynamic_index_in_dim(selection, me, 0, keepdims=False) // blk_dev
    got = [
        lax.all_to_all(
            cache.reshape(blk_dev, BLOCK, -1)[inner], "seq", split_axis=0, concat_axis=0, tiled=True
        )
        for cache in (key_cache, value_cache)
    ]
    q_pieces, k_pieces, v_pieces = spread(queries), spread(new_keys), spread(new_values)
    from_of = jnp.stack([group] + [lax.rem(group + b, n) for b in range(n, 0, -1)]).astype(jnp.int32)
    per = 2 if heads % 2 == 0 else 1
    cols = per * HD
    own = pl.BlockSpec((rows, cols), lambda h, w, o: (0, w[0] * (heads // per) + h))
    other = pl.BlockSpec((rows, cols), lambda h, w, o: (0, h))
    cached = [
        pl.BlockSpec((1, BLOCK, cols), functools.partial(lambda t, h, w, o: (o[t], 0, h), t))
        for t in range(topk)
    ]
    count = rows * n
    out = pl.pallas_call(
        functools.partial(
            ulysses_kernel, n, topk, per, 2, float(HD) ** (-0.5) * LOG2E
        ),
        out_shape=jax.ShapeDtypeStruct((count, width), jnp.bfloat16),
        grid_spec=pltpu.PrefetchScalarGridSpec(
            num_scalar_prefetch=2,
            grid=(heads // per,),
            in_specs=([own] + [other] * (n - 1)) * 3 + cached * 2,
            out_specs=pl.BlockSpec((count, cols), lambda h, w, o: (0, h)),
            scratch_shapes=[pltpu.VMEM((count, cols), jnp.bfloat16)] * 3,
        ),
        name="attend",
    )(from_of, mine, *q_pieces, *k_pieces, *v_pieces, *([got[0]] * topk), *([got[1]] * topk))
    result = jnp.zeros((rows, features), jnp.bfloat16)
    for b in range(n):
        piece = lax.dynamic_slice_in_dim(out, peer(b) * rows, rows, axis=0)
        if b > 0:
            piece = exchange(b, piece)
        result = lax.dynamic_update_slice_in_dim(
            result, piece, lax.rem(group + n - b, n) * width, axis=1
        )
    return result


def chip_bias(bias, place, rows):
    def token(at):
        return jnp.where(at < rows, place * rows + at, (1 - place) * rows + at - rows)

    q = token(lax.broadcasted_iota(jnp.int32, bias.shape, 0))
    k = lax.broadcasted_iota(jnp.int32, bias.shape, 1)
    bias[...] = jnp.where((k >= 2 * rows) | (q >= token(k)), 0.0, MASKED)


def biased(scores, seen, bias):
    masked = min(bias.shape[1], scores.shape[1] - seen)
    parts = [scores[:, seen : seen + masked] + bias[:, :masked]]
    if seen > 0:
        parts.insert(0, scores[:, :seen])
    if scores.shape[1] > seen + masked:
        parts.append(scores[:, seen + masked :])
    return jnp.concatenate(parts, axis=1)


def soft(scores, values):
    top = jnp.max(scores, axis=1, keepdims=True)
    weights = jnp.exp2(scores - top)
    total = jnp.sum(weights, axis=1, keepdims=True)
    mixed = jnp.dot(weights.astype(jnp.bfloat16), values, preferred_element_type=jnp.float32)
    return mixed, top, total


def held(sel_ref, row, owner, blk_dev):
    inner = jnp.int32(0)
    for t in range(sel_ref.shape[0]):
        picked = sel_ref[t, row]
        match = lax.div(picked, jnp.int32(blk_dev)) == owner
        inner = jnp.where(match, lax.rem(picked, jnp.int32(blk_dev)), inner)
    return inner


def group_index():
    return lax.axis_index("head") * 2 + lax.axis_index("sub")


def run_copies(pairs, sems):
    copies = [pltpu.make_async_copy(a, b, sems.at[i]) for i, (a, b) in enumerate(pairs)]
    for copy in copies:
        copy.start()
    for copy in copies:
        copy.wait()


def cross_kernel(width, start, size, q, k, v, after, *refs):
    outs, sems = refs[:-1], refs[-1]

    def pairs(arrays, outs):
        result = []
        for out, d in zip(outs, (2, 3)):
            at = (group_index() ^ d) * width + start
            cols = pl.ds(pl.multiple_of(at, HD), size)
            for i, array in enumerate(arrays):
                result.append((array.at[:, cols], out.at[:, i * size : (i + 1) * size]))
        return result

    @pl.when(lax.axis_index("head") == 0)
    def _():
        run_copies(pairs((k, v), outs), sems)

    @pl.when(lax.axis_index("head") == 1)
    def _():
        run_copies(pairs((q, q), outs), sems)


def core_kernel(width, start, size, flip, q, k, v, after, out, sems):
    pairs = []
    for i in range(2):
        at = (2 * i + (lax.axis_index("sub") ^ flip)) * width + start
        cols = pl.ds(pl.multiple_of(at, HD), size)
        for t, array in enumerate((q, k, v)):
            to = (3 * i + t) * size
            pairs.append((array.at[:, cols], out.at[:, to : to + size]))
    run_copies(pairs, sems)


def sends_kernel(n_seq, blk_dev, rows, chunks, sel_ref, kc, vc, *refs):
    outs, bias, sems = refs[:-2], refs[-2], refs[-1]
    me = lax.axis_index("seq")
    pairs = []
    for i, (start, size) in enumerate(chunks):
        for d in range(n_seq):
            inner = held(sel_ref, me ^ d, me, blk_dev)
            at = pl.ds(pl.multiple_of(inner * BLOCK, BLOCK), BLOCK)
            to = outs[i * n_seq + d]
            pairs.append((kc.at[at, start : start + size], to.at[:BLOCK]))
            pairs.append((vc.at[at, start : start + size], to.at[BLOCK:]))
    copies = [pltpu.make_async_copy(a, b, sems.at[i]) for i, (a, b) in enumerate(pairs)]
    for copy in copies:
        copy.start()
    chip_bias(bias, lax.axis_index("sub"), rows)
    for copy in copies:
        copy.wait()


def collect_kernel(blk_dev, sel_ref, *refs):
    sources, kept = refs[:-1], refs[-1]
    me = lax.axis_index("seq")
    topk = sel_ref.shape[0]
    for t in range(topk):
        distance = lax.div(sel_ref[t, me], jnp.int32(blk_dev)) ^ me
        for d, source in enumerate(sources):

            @pl.when(distance == d)
            def _():
                kept[t * BLOCK : (t + 1) * BLOCK] = source[:BLOCK]
                kept[(topk + t) * BLOCK : (topk + t + 1) * BLOCK] = source[BLOCK:]


def lane_put(into, lane, column):
    lanes = lax.broadcasted_iota(jnp.int32, into.shape, 1)
    return jnp.where(lanes == lane, column, into)


def column(stat, lane):
    lanes = lax.broadcasted_iota(jnp.int32, stat.shape, 1)
    return jnp.sum(jnp.where(lanes == lane, stat, 0.0), axis=1, keepdims=True)


def resume(scores, values, mixed, top, total):
    here = jnp.maximum(jnp.max(scores, axis=1, keepdims=True), top)
    weights = jnp.exp2(scores - here)
    carry = jnp.exp2(top - here)
    total = jnp.sum(weights, axis=1, keepdims=True) + total * carry
    more = jnp.dot(weights.astype(jnp.bfloat16), values, preferred_element_type=jnp.float32)
    return more + mixed * carry, here, total


class Rows:
    def __init__(self, size, first, second):
        self.size, self.refs, self.rows = size, (first, second), first.shape[0]

    def clear(self):
        for ref in self.refs:
            ref[:, self.size :] = jnp.zeros((self.rows, HD), jnp.float32)

    def put(self, col, mixed):
        for i, ref in enumerate(self.refs):
            ref[:, col] = mixed[i * self.rows : (i + 1) * self.rows].astype(ref.dtype)

    def put_stat(self, head, top, total):
        for i, ref in enumerate(self.refs):
            at = slice(i * self.rows, (i + 1) * self.rows)
            stat = lane_put(ref[:, self.size :], 2 * head, top[at])
            ref[:, self.size :] = lane_put(stat, 2 * head + 1, total[at])

    def get(self, col, head):
        mixed = jnp.concatenate([ref[:, col] for ref in self.refs], axis=0)
        stat = jnp.concatenate([ref[:, self.size :] for ref in self.refs], axis=0)
        return mixed, column(stat, 2 * head), column(stat, 2 * head + 1)


def each_head(per, size, work):
    def step(h, carry):
        for j in range(per):
            head = h * per + j
            work(head, pl.ds(pl.multiple_of(head * HD, HD), HD))
        return carry

    lax.fori_loop(0, size // HD // per, step, 0)


def part_of(refs, size, t, head):
    at = pl.ds(pl.multiple_of(t * size + head * HD, HD), HD)
    return [ref[:, at] for ref in refs]


def rows_of(refs, size, t, head):
    return jnp.concatenate(part_of(refs, size, t, head), axis=0)


def span_kernel(per, size, factor, bias, own, par, a0, a1, b0, b1):
    def work(head, col):
        for base, rows in ((0, first), (3, second)):
            k, v = (rows_of((own, par), size, base + t, head) for t in (1, 2))
            scores = logits(rows_of((own, par), size, base, head), k, factor)
            mixed, top, total = soft(biased(scores, 0, bias), v)
            rows.put(col, mixed)
            rows.put_stat(head, top, total)

    first, second = Rows(size, a0, a1), Rows(size, b0, b1)
    first.clear()
    second.clear()
    each_head(per, size, work)


def other_kernel(per, size, factor, own, par, two, three, b0, b1, s0, s1):
    second, result = Rows(size, b0, b1), Rows(size, s0, s1)
    result.clear()

    def keep(head, col, mixed, top, total):
        result.put(col, mixed)
        result.put_stat(head, top, total)

    def on_first(head, col):
        k, v = (rows_of((own, par), size, t, head) for t in (1, 2))
        keep(head, col, *soft(logits(rows_of((two, three), size, 0, head), k, factor), v))

    def on_second(head, col):
        k, v = (rows_of((two, three), size, t, head) for t in (0, 1))
        scores = logits(rows_of((own, par), size, 3, head), k, factor)
        keep(head, col, *resume(scores, v, *second.get(col, head)))

    @pl.when(lax.axis_index("head") == 0)
    def _():
        each_head(per, size, on_first)

    @pl.when(lax.axis_index("head") == 1)
    def _():
        each_head(per, size, on_second)


def early_kernel(per, size, factor, own, par, two, three, kept, a0, a1, p0, p1, loc0, loc1, part0, part1):
    heads = size // HD
    first, partial = Rows(size, a0, a1), Rows(size, p0, p1)
    loc, part = Rows(size, loc0, loc1), Rows(size, part0, part1)

    def on_first(head, col):
        k, v = kept[: 2 * BLOCK, col], kept[2 * BLOCK :, col]
        scores = logits(rows_of((own, par), size, 0, head), k, factor)
        mixed, top, total = resume(scores, v, *first.get(col, head))
        loc.put(col, mixed * (1.0 / total))
        scores = logits(rows_of((two, three), size, 0, head), k, factor)
        mixed, top, total = resume(scores, v, *partial.get(col, head))
        part.put(col, mixed * (1.0 / total))
        loc.put_stat(head, top, total)

    @pl.when(lax.axis_index("head") == 0)
    def _():
        loc.clear()
        each_head(per, size, on_first)
        for source, into in zip(loc.refs, part.refs):
            left = source[:, size:]
            packed = jnp.zeros_like(left)
            for t in range(3):
                piece = left.astype(jnp.bfloat16).astype(jnp.float32)
                left = left - piece
                packed = packed + (pltpu.roll(piece, 2 * heads * t, 1) if t > 0 else piece)
            into[:, size:] = packed.astype(jnp.bfloat16)

    @pl.when(lax.axis_index("head") == 1)
    def _():
        for source, into in zip(first.refs, loc.refs):
            into[...] = source[...]


def late_kernel(per, size, factor, own, par, kept, crossed, b0, b1, s0, s1, out0, out1):
    out = Rows(size, out0, out1)

    def run(cache, second):
        def work(head, col):
            scores = logits(rows_of((own, par), size, 3, head), cache[: 2 * BLOCK, col], factor)
            mixed, _, total = resume(scores, cache[2 * BLOCK :, col], *second.get(col, head))
            out.put(col, mixed * (1.0 / total))

        each_head(per, size, work)

    @pl.when(lax.axis_index("head") == 0)
    def _():
        run(crossed, Rows(size, b0, b1))

    @pl.when(lax.axis_index("head") == 1)
    def _():
        run(kept, Rows(size, s0, s1))


def finish_kernel(width, start, size, count, *refs):
    own, got, loc_own, loc_got, far_own, far_got = refs[:6]
    result, merged_own, merged_got, sems = refs[count:]
    heads = size // HD
    c = lax.axis_index("sub")

    def put(array, group, i):
        to = pl.ds(pl.multiple_of(group * width + start, HD), size)
        return pltpu.make_async_copy(array, result.at[:, to], sems.at[i])

    copies = [put(own, 2 + c, 0), put(got, 3 - c, 1)]
    for copy in copies:
        copy.start()
    pairs = ((loc_own, far_own, merged_own), (loc_got, far_got, merged_got))

    @pl.when(lax.axis_index("head") == 0)
    def _():
        for loc, far, merged in pairs:
            merged[...] = loc[:, :size].astype(jnp.bfloat16)

    @pl.when(lax.axis_index("head") == 1)
    def _():
        for loc, far, merged in pairs:
            packed = far[:, size:].astype(jnp.float32)
            there = packed
            for t in range(1, 3):
                there = there + pltpu.roll(packed, HD - 2 * heads * t, 1)
            here = loc[:, size:]
            for i in range(heads):
                col = slice(i * HD, (i + 1) * HD)
                near_top, near_sum = here[:, 2 * i : 2 * i + 1], here[:, 2 * i + 1 : 2 * i + 2]
                far_top, far_sum = there[:, 2 * i : 2 * i + 1], there[:, 2 * i + 1 : 2 * i + 2]
                top = jnp.maximum(near_top, far_top)
                near = jnp.exp2(near_top - top)
                away = far_sum * jnp.exp2(far_top - top)
                scale = 1.0 / (near_sum * near + away)
                mixed = loc[:, col] * (near * scale)
                mixed = mixed + far[:, col].astype(jnp.float32) * (away * scale)
                merged[:, col] = mixed.astype(jnp.bfloat16)

    copies += [put(merged_own, c, 2), put(merged_got, 1 - c, 3)]
    for copy in copies[2:]:
        copy.start()
    for copy in copies:
        copy.wait()


def hybrid(n_seq, chunk_heads, queries, new_keys, new_values, key_cache, value_cache, selection):
    n = 4
    rows, features = queries.shape
    width = features // n
    heads = width // HD
    chunks, first = [], 0
    for count in chunk_heads(heads):
        chunks.append((first * HD, count * HD))
        first += count
    factor = float(HD) ** (-0.5) * LOG2E
    blk_dev = key_cache.shape[0] // BLOCK
    picks = pltpu.with_memory_space_constraint(selection.T, pltpu.HBM)
    anywhere = pl.BlockSpec(memory_space=pl.ANY)
    in_hbm = pl.BlockSpec(memory_space=pltpu.HBM)
    resident = pl.BlockSpec(memory_space=pltpu.VMEM)
    bf16, f32 = jnp.bfloat16, jnp.float32

    def call(kernel, arrays, in_specs, shapes, scratch=(), scalars=(), result=None):
        return pl.pallas_call(
            kernel,
            out_shape=[pltpu.VMEM(*s) for s in shapes] if result is None else result,
            grid_spec=pltpu.PrefetchScalarGridSpec(
                num_scalar_prefetch=len(scalars),
                grid=(1,),
                in_specs=in_specs,
                out_specs=[resident] * len(shapes) if result is None else anywhere,
                scratch_shapes=list(scratch),
            ),
            input_output_aliases={6: 0} if len(arrays) == 7 and result is not None else {},
            compiler_params=pltpu.CompilerParams(vmem_limit_bytes=VMEM_LIMIT),
        )(*scalars, *arrays)

    def move(x, pairs, axes=("head", "sub")):
        return lax.ppermute(x, axes, list(pairs))

    def apart(d, sources=range(n)):
        return [(i, i ^ d) for i in sources]

    arrays = [pltpu.with_memory_space_constraint(x, pltpu.HBM) for x in (queries, new_keys, new_values)]
    caches = [pltpu.with_memory_space_constraint(x, pltpu.HBM) for x in (key_cache, value_cache)]
    from_args = [in_hbm] * 3 + [anywhere]

    def cross(i, after):
        start, size = chunks[i]
        sent = call(
            functools.partial(cross_kernel, width, start, size), arrays + [after],
            from_args, [((rows, 2 * size), bf16)] * 2, [pltpu.SemaphoreType.DMA((4,))],
        )
        return sent, [move(sent[d - 2], apart(d)) for d in (2, 3)]

    def cores(i, flip, after):
        start, size = chunks[i]
        return call(
            functools.partial(core_kernel, width, start, size, flip),
            arrays + [after], from_args, [((rows, 6 * size), bf16)],
            [pltpu.SemaphoreType.DMA((6,))],
        )[0]

    sends = call(
        functools.partial(sends_kernel, n_seq, blk_dev, rows, chunks),
        caches, [in_hbm] * 2,
        [((2 * BLOCK, size), bf16) for _, size in chunks for _ in range(n_seq)]
        + [((2 * rows, pl.cdiv(2 * rows, HD) * HD), f32)],
        [pltpu.SemaphoreType.DMA((2 * n_seq * len(chunks),))], [picks],
    )
    bias = sends[-1]
    sent, crossing = [sends[1]], []
    for i in range(len(chunks)):
        sent, came = cross(i, sent[0])
        crossing.append(came)
    own, par, after = [], [], sent[0]
    for i in range(len(chunks)):
        after = cores(i, 1, after)
        par.append(move(after, apart(1)))
    for i in range(len(chunks)):
        after = cores(i, 0, after)
        own.append(after)

    def fetch(i):
        block = sends[n_seq * i : n_seq * (i + 1)]
        came = [block[0]]
        for d in range(1, n_seq):
            came.append(move(block[d], [(z, z ^ d) for z in range(n_seq)], "seq"))
        kept = call(
            functools.partial(collect_kernel, blk_dev), came, [resident] * n_seq,
            [((4 * BLOCK, chunks[i][1]), bf16)], (), [picks],
        )[0]
        return kept, move(kept, apart(2, (2, 3)))

    result = None
    for i, (start, size) in enumerate(chunks):
        kept, crossed = fetch(i)
        per = 2 if size // HD % 2 == 0 else 1
        both = [own[i], par[i]]
        held_f32, held_bf16 = ((rows, size + HD), f32), ((rows, size + HD), bf16)
        a0, a1, b0, b1 = call(
            functools.partial(span_kernel, per, size, factor), [bias] + both,
            [resident] * 3, [held_f32] * 4,
        )
        s0, s1 = call(
            functools.partial(other_kernel, per, size, factor),
            both + crossing[i] + [b0, b1], [resident] * 6, [held_f32] * 2,
        )
        loc0, loc1, part0, part1 = call(
            functools.partial(early_kernel, per, size, factor),
            both + crossing[i] + [kept, a0, a1, s0, s1], [resident] * 9,
            [held_f32] * 2 + [held_bf16] * 2,
        )
        far0 = move(part0, apart(2, (0, 1)))
        far1 = move(part1, apart(3, (0, 1)))
        got_loc = move(loc1, apart(1))
        out0, out1 = call(
            functools.partial(late_kernel, per, size, factor),
            both + [kept, crossed, b0, b1, s0, s1], [resident] * 8, [((rows, size), bf16)] * 2,
        )
        got = move(out1, apart(1))
        pieces = [out0, got, loc0, got_loc, far0, far1]
        specs = [resident] * 6
        if result is not None:
            pieces, specs = pieces + [result], specs + [anywhere]
        result = call(
            functools.partial(finish_kernel, width, start, size, len(pieces)),
            pieces, specs, [],
            [pltpu.VMEM((rows, size), bf16)] * 2 + [pltpu.SemaphoreType.DMA((4,))],
            (), jax.ShapeDtypeStruct((rows, features), bf16),
        )
    return result


def uneven(heads):
    second = max(2, heads * 3 // 8 // 2 * 2)
    return (heads - second, second)


def placed_map(body, mesh, placed):
    return jax.shard_map(
        body,
        mesh=mesh,
        in_specs=placed,
        out_specs=P(("groups", "seq", "head", "sub"), None),
        check_vma=False,
    )


def solution(mesh):
    subs = mesh.shape["sub"]
    n = mesh.shape["head"] * subs
    placed = (
        P(("groups", "seq", "head", "sub"), None),
        P(("groups", "seq", "head", "sub"), None),
        P(("groups", "seq", "head", "sub"), None),
        P(("groups", "seq"), ("head", "sub")),
        P(("groups", "seq"), ("head", "sub")),
        P("groups", None),
    )
    n_seq = mesh.shape["seq"]
    body = functools.partial(ulysses, n, subs)
    if (mesh.shape["head"], subs, n_seq) == (2, 2, 4):
        body = functools.partial(hybrid, n_seq, uneven)
    if (mesh.shape["head"], subs, n_seq) != (2, 2, 4):
        return placed_map(body, mesh, placed)

    def step(*args):
        return body(*args)

    return placed_map(step, mesh, placed)
```

```python
import functools

import jax
import jax.numpy as jnp
from jax import lax
from jax.experimental import pallas as pl
from jax.experimental.pallas import tpu as pltpu
from jax.sharding import PartitionSpec as P


HD = 128
BLOCK = 64
LOG2E = 1.4426950408889634
MASKED = -1e30
VMEM_LIMIT = 16 << 20


def softmax_rows(scores, values):
    top = functools.reduce(jnp.maximum, [jnp.max(s, axis=1, keepdims=True) for s in scores])
    weights = [jnp.exp2(s - top) for s in scores]
    total = functools.reduce(jnp.add, [jnp.sum(w, axis=1, keepdims=True) for w in weights])
    mixed = functools.reduce(
        jnp.add,
        [
            jnp.dot(w.astype(jnp.bfloat16), v, preferred_element_type=jnp.float32)
            for w, v in zip(weights, values)
        ],
    )
    return mixed, top, total


def logits(q, k, factor):
    return lax.dot_general(
        q, k, (((1,), (1,)), ((), ())), preferred_element_type=jnp.float32
    ) * factor


def ulysses_kernel(n, topk, per, parts, factor, where_ref, own_ref, *refs):
    qs, ks, vs = refs[:n], refs[n : 2 * n], refs[2 * n : 3 * n]
    cks, cvs = refs[3 * n : 3 * n + topk], refs[3 * n + topk : 3 * n + 2 * topk]
    out_ref, q_all, k_all, v_all = refs[3 * n + 2 * topk :]
    rows = qs[0].shape[0]
    count = rows * n
    for b in range(n):
        at = pl.ds(pl.multiple_of(where_ref[1 + b] * rows, rows), rows)
        q_all[at, :] = qs[b][...]
        k_all[at, :] = ks[b][...]
        v_all[at, :] = vs[b][...]
    step = count // parts
    causal = lax.broadcasted_iota(jnp.int32, (step, step), 0) >= lax.broadcasted_iota(
        jnp.int32, (step, step), 1
    )
    for j in range(per):
        col = slice(j * HD, (j + 1) * HD)
        ck = [r[0, :, col] for r in cks]
        cv = [r[0, :, col] for r in cvs]
        ck = jnp.concatenate(ck, axis=0)
        cv = jnp.concatenate(cv, axis=0)
        for i in range(parts):
            here = slice(i * step, (i + 1) * step)
            q = q_all[here, col]
            scores = [logits(q, ck, factor)]
            values = [cv]
            if i > 0:
                scores.append(logits(q, k_all[: i * step, col], factor))
                values.append(v_all[: i * step, col])
            scores.append(jnp.where(causal, logits(q, k_all[here, col], factor), MASKED))
            values.append(v_all[here, col])
            mixed, _, total = softmax_rows(scores, values)
            out_ref[here, col] = (mixed / total).astype(jnp.bfloat16)


def ulysses(n, subs, queries, new_keys, new_values, key_cache, value_cache, selection):
    rows, features = queries.shape
    width = features // n
    heads = width // HD
    topk = selection.shape[1]
    me = lax.axis_index("seq")
    group = lax.axis_index("head") * subs + lax.axis_index("sub")

    def peer(b):
        return lax.rem(group + b, n)

    def exchange(b, piece):
        return lax.ppermute(piece, ("head", "sub"), [(i, (i + b) % n) for i in range(n)])

    def spread(array):
        pieces = [array]
        for b in range(1, n):
            piece = lax.dynamic_slice_in_dim(array, peer(b) * width, width, axis=1)
            pieces.append(exchange(b, piece))
        return pieces

    blk_dev = key_cache.shape[0] // BLOCK
    owner_of = selection // blk_dev
    inner = jnp.sum(jnp.where(owner_of == me, selection % blk_dev, 0), axis=1)
    mine = lax.dynamic_index_in_dim(selection, me, 0, keepdims=False) // blk_dev
    got = [
        lax.all_to_all(
            cache.reshape(blk_dev, BLOCK, -1)[inner], "seq", split_axis=0, concat_axis=0, tiled=True
        )
        for cache in (key_cache, value_cache)
    ]
    q_pieces, k_pieces, v_pieces = spread(queries), spread(new_keys), spread(new_values)
    from_of = jnp.stack([group] + [lax.rem(group + b, n) for b in range(n, 0, -1)]).astype(jnp.int32)
    per = 2 if heads % 2 == 0 else 1
    cols = per * HD
    own = pl.BlockSpec((rows, cols), lambda h, w, o: (0, w[0] * (heads // per) + h))
    other = pl.BlockSpec((rows, cols), lambda h, w, o: (0, h))
    cached = [
        pl.BlockSpec((1, BLOCK, cols), functools.partial(lambda t, h, w, o: (o[t], 0, h), t))
        for t in range(topk)
    ]
    count = rows * n
    out = pl.pallas_call(
        functools.partial(
            ulysses_kernel, n, topk, per, 2, float(HD) ** (-0.5) * LOG2E
        ),
        out_shape=jax.ShapeDtypeStruct((count, width), jnp.bfloat16),
        grid_spec=pltpu.PrefetchScalarGridSpec(
            num_scalar_prefetch=2,
            grid=(heads // per,),
            in_specs=([own] + [other] * (n - 1)) * 3 + cached * 2,
            out_specs=pl.BlockSpec((count, cols), lambda h, w, o: (0, h)),
            scratch_shapes=[pltpu.VMEM((count, cols), jnp.bfloat16)] * 3,
        ),
        name="attend",
    )(from_of, mine, *q_pieces, *k_pieces, *v_pieces, *([got[0]] * topk), *([got[1]] * topk))
    result = jnp.zeros((rows, features), jnp.bfloat16)
    for b in range(n):
        piece = lax.dynamic_slice_in_dim(out, peer(b) * rows, rows, axis=0)
        if b > 0:
            piece = exchange(b, piece)
        result = lax.dynamic_update_slice_in_dim(
            result, piece, lax.rem(group + n - b, n) * width, axis=1
        )
    return result


def chip_bias(bias, place, rows):
    def token(at):
        return jnp.where(at < rows, place * rows + at, (1 - place) * rows + at - rows)

    q = token(lax.broadcasted_iota(jnp.int32, bias.shape, 0))
    k = lax.broadcasted_iota(jnp.int32, bias.shape, 1)
    bias[...] = jnp.where((k >= 2 * rows) | (q >= token(k)), 0.0, MASKED)


def biased(scores, seen, bias):
    masked = min(bias.shape[1], scores.shape[1] - seen)
    parts = [scores[:, seen : seen + masked] + bias[:, :masked]]
    if seen > 0:
        parts.insert(0, scores[:, :seen])
    if scores.shape[1] > seen + masked:
        parts.append(scores[:, seen + masked :])
    return jnp.concatenate(parts, axis=1)


def soft(scores, values):
    top = jnp.max(scores, axis=1, keepdims=True)
    weights = jnp.exp2(scores - top)
    total = jnp.sum(weights, axis=1, keepdims=True)
    mixed = jnp.dot(weights.astype(jnp.bfloat16), values, preferred_element_type=jnp.float32)
    return mixed, top, total


def held(sel_ref, row, owner, blk_dev):
    inner = jnp.int32(0)
    for t in range(sel_ref.shape[0]):
        picked = sel_ref[t, row]
        match = lax.div(picked, jnp.int32(blk_dev)) == owner
        inner = jnp.where(match, lax.rem(picked, jnp.int32(blk_dev)), inner)
    return inner


def group_index():
    return lax.axis_index("head") * 2 + lax.axis_index("sub")


def run_copies(pairs, sems):
    copies = [pltpu.make_async_copy(a, b, sems.at[i]) for i, (a, b) in enumerate(pairs)]
    for copy in copies:
        copy.start()
    for copy in copies:
        copy.wait()


def cross_kernel(width, chunk, asked, q, k, v, after, two, three, sems):
    def pairs(wanted):
        result = []
        for out, d in ((two, 2), (three, 3)):
            to = 0
            for array, (start, size) in wanted:
                at = (group_index() ^ d) * width + start
                cols = pl.ds(pl.multiple_of(at, HD), size)
                result.append((array.at[:, cols], out.at[:, to : to + size]))
                to += size
        return result

    @pl.when(lax.axis_index("head") == 0)
    def _():
        run_copies(pairs([(k, chunk), (v, chunk)]), sems)

    @pl.when(lax.axis_index("head") == 1)
    def _():
        run_copies(pairs([(q, other) for other in asked]), sems)


def core_kernel(width, start, size, flip, q, k, v, after, out, sems):
    pairs = []
    for i in range(2):
        at = (2 * i + (lax.axis_index("sub") ^ flip)) * width + start
        cols = pl.ds(pl.multiple_of(at, HD), size)
        for t, array in enumerate((q, k, v)):
            to = (3 * i + t) * size
            pairs.append((array.at[:, cols], out.at[:, to : to + size]))
    run_copies(pairs, sems)


def sends_kernel(n_seq, blk_dev, rows, chunks, sel_ref, kc, vc, *refs):
    outs, bias, sems = refs[:-2], refs[-2], refs[-1]
    me = lax.axis_index("seq")
    pairs = []
    for i, (start, size) in enumerate(chunks):
        for d in range(n_seq):
            inner = held(sel_ref, me ^ d, me, blk_dev)
            at = pl.ds(pl.multiple_of(inner * BLOCK, BLOCK), BLOCK)
            to = outs[i * n_seq + d]
            pairs.append((kc.at[at, start : start + size], to.at[:BLOCK]))
            pairs.append((vc.at[at, start : start + size], to.at[BLOCK:]))
    copies = [pltpu.make_async_copy(a, b, sems.at[i]) for i, (a, b) in enumerate(pairs)]
    for copy in copies:
        copy.start()
    chip_bias(bias, lax.axis_index("sub"), rows)
    for copy in copies:
        copy.wait()


def collect_kernel(blk_dev, sel_ref, *refs):
    sources, kept = refs[:-1], refs[-1]
    me = lax.axis_index("seq")
    topk = sel_ref.shape[0]
    for t in range(topk):
        distance = lax.div(sel_ref[t, me], jnp.int32(blk_dev)) ^ me
        for d, source in enumerate(sources):

            @pl.when(distance == d)
            def _():
                kept[t * BLOCK : (t + 1) * BLOCK] = source[:BLOCK]
                kept[(topk + t) * BLOCK : (topk + t + 1) * BLOCK] = source[BLOCK:]


def lane_put(into, lane, column):
    lanes = lax.broadcasted_iota(jnp.int32, into.shape, 1)
    return jnp.where(lanes == lane, column, into)


def column(stat, lane):
    lanes = lax.broadcasted_iota(jnp.int32, stat.shape, 1)
    return jnp.sum(jnp.where(lanes == lane, stat, 0.0), axis=1, keepdims=True)


def resume(scores, values, mixed, top, total):
    here = jnp.maximum(jnp.max(scores, axis=1, keepdims=True), top)
    weights = jnp.exp2(scores - here)
    carry = jnp.exp2(top - here)
    total = jnp.sum(weights, axis=1, keepdims=True) + total * carry
    more = jnp.dot(weights.astype(jnp.bfloat16), values, preferred_element_type=jnp.float32)
    return more + mixed * carry, here, total


class Rows:
    def __init__(self, size, first, second):
        self.size, self.refs, self.rows = size, (first, second), first.shape[0]

    def clear(self):
        for ref in self.refs:
            ref[:, self.size :] = jnp.zeros((self.rows, HD), jnp.float32)

    def put(self, col, mixed):
        for i, ref in enumerate(self.refs):
            ref[:, col] = mixed[i * self.rows : (i + 1) * self.rows].astype(ref.dtype)

    def put_stat(self, head, top, total):
        for i, ref in enumerate(self.refs):
            at = slice(i * self.rows, (i + 1) * self.rows)
            stat = lane_put(ref[:, self.size :], 2 * head, top[at])
            ref[:, self.size :] = lane_put(stat, 2 * head + 1, total[at])

    def get(self, col, head):
        mixed = jnp.concatenate([ref[:, col] for ref in self.refs], axis=0)
        stat = jnp.concatenate([ref[:, self.size :] for ref in self.refs], axis=0)
        return mixed, column(stat, 2 * head), column(stat, 2 * head + 1)


def each_head(per, size, work):
    def step(h, carry):
        for j in range(per):
            head = h * per + j
            work(head, pl.ds(pl.multiple_of(head * HD, HD), HD))
        return carry

    lax.fori_loop(0, size // HD // per, step, 0)


def part_of(refs, size, t, head):
    at = pl.ds(pl.multiple_of(t * size + head * HD, HD), HD)
    return [ref[:, at] for ref in refs]


def rows_of(refs, size, t, head):
    return jnp.concatenate(part_of(refs, size, t, head), axis=0)


def span_kernel(per, size, factor, bias, own, par, a0, a1, b0, b1):
    def work(head, col):
        for base, rows in ((0, first), (3, second)):
            k, v = (rows_of((own, par), size, base + t, head) for t in (1, 2))
            scores = logits(rows_of((own, par), size, base, head), k, factor)
            mixed, top, total = soft(biased(scores, 0, bias), v)
            rows.put(col, mixed)
            rows.put_stat(head, top, total)

    first, second = Rows(size, a0, a1), Rows(size, b0, b1)
    first.clear()
    second.clear()
    each_head(per, size, work)


def other_kernel(per, size, asked_at, factor, own, par, two, three, q_two, q_three, b0, b1, s0, s1):
    second, result = Rows(size, b0, b1), Rows(size, s0, s1)
    result.clear()

    def keep(head, col, mixed, top, total):
        result.put(col, mixed)
        result.put_stat(head, top, total)

    def on_first(head, col):
        k, v = (rows_of((own, par), size, t, head) for t in (1, 2))
        q = rows_of((q_two, q_three), asked_at, 1, head)
        keep(head, col, *soft(logits(q, k, factor), v))

    def on_second(head, col):
        k, v = (rows_of((two, three), size, t, head) for t in (0, 1))
        scores = logits(rows_of((own, par), size, 3, head), k, factor)
        keep(head, col, *resume(scores, v, *second.get(col, head)))

    @pl.when(lax.axis_index("head") == 0)
    def _():
        each_head(per, size, on_first)

    @pl.when(lax.axis_index("head") == 1)
    def _():
        each_head(per, size, on_second)


def early_kernel(per, size, asked_at, factor, own, par, q_two, q_three, kept, a0, a1, p0, p1, loc0, loc1, part0, part1):
    heads = size // HD
    first, partial = Rows(size, a0, a1), Rows(size, p0, p1)
    loc, part = Rows(size, loc0, loc1), Rows(size, part0, part1)

    def on_first(head, col):
        k, v = kept[: 2 * BLOCK, col], kept[2 * BLOCK :, col]
        scores = logits(rows_of((own, par), size, 0, head), k, factor)
        mixed, top, total = resume(scores, v, *first.get(col, head))
        loc.put(col, mixed * (1.0 / total))
        scores = logits(rows_of((q_two, q_three), asked_at, 1, head), k, factor)
        mixed, top, total = resume(scores, v, *partial.get(col, head))
        part.put(col, mixed * (1.0 / total))
        loc.put_stat(head, top, total)

    @pl.when(lax.axis_index("head") == 0)
    def _():
        loc.clear()
        each_head(per, size, on_first)
        for source, into in zip(loc.refs, part.refs):
            left = source[:, size:]
            packed = jnp.zeros_like(left)
            for t in range(3):
                piece = left.astype(jnp.bfloat16).astype(jnp.float32)
                left = left - piece
                packed = packed + (pltpu.roll(piece, 2 * heads * t, 1) if t > 0 else piece)
            into[:, size:] = packed.astype(jnp.bfloat16)

    @pl.when(lax.axis_index("head") == 1)
    def _():
        for source, into in zip(first.refs, loc.refs):
            into[...] = source[...]


def late_kernel(per, size, factor, own, par, kept, crossed, b0, b1, s0, s1, out0, out1):
    out = Rows(size, out0, out1)

    def run(cache, second):
        def work(head, col):
            scores = logits(rows_of((own, par), size, 3, head), cache[: 2 * BLOCK, col], factor)
            mixed, _, total = resume(scores, cache[2 * BLOCK :, col], *second.get(col, head))
            out.put(col, mixed * (1.0 / total))

        each_head(per, size, work)

    @pl.when(lax.axis_index("head") == 0)
    def _():
        run(crossed, Rows(size, b0, b1))

    @pl.when(lax.axis_index("head") == 1)
    def _():
        run(kept, Rows(size, s0, s1))


def finish_kernel(width, start, size, count, *refs):
    own, got, loc_own, loc_got, far_own, far_got = refs[:6]
    result, merged_own, merged_got, sems = refs[count:]
    heads = size // HD
    c = lax.axis_index("sub")

    def put(array, group, i):
        to = pl.ds(pl.multiple_of(group * width + start, HD), size)
        return pltpu.make_async_copy(array, result.at[:, to], sems.at[i])

    copies = [put(own, 2 + c, 0), put(got, 3 - c, 1)]
    for copy in copies:
        copy.start()
    pairs = ((loc_own, far_own, merged_own), (loc_got, far_got, merged_got))

    @pl.when(lax.axis_index("head") == 0)
    def _():
        for loc, far, merged in pairs:
            merged[...] = loc[:, :size].astype(jnp.bfloat16)

    @pl.when(lax.axis_index("head") == 1)
    def _():
        for loc, far, merged in pairs:
            packed = far[:, size:].astype(jnp.float32)
            there = packed
            for t in range(1, 3):
                there = there + pltpu.roll(packed, HD - 2 * heads * t, 1)
            here = loc[:, size:]
            for i in range(heads):
                col = slice(i * HD, (i + 1) * HD)
                near_top, near_sum = here[:, 2 * i : 2 * i + 1], here[:, 2 * i + 1 : 2 * i + 2]
                far_top, far_sum = there[:, 2 * i : 2 * i + 1], there[:, 2 * i + 1 : 2 * i + 2]
                top = jnp.maximum(near_top, far_top)
                near = jnp.exp2(near_top - top)
                away = far_sum * jnp.exp2(far_top - top)
                scale = 1.0 / (near_sum * near + away)
                mixed = loc[:, col] * (near * scale)
                mixed = mixed + far[:, col].astype(jnp.float32) * (away * scale)
                merged[:, col] = mixed.astype(jnp.bfloat16)

    copies += [put(merged_own, c, 2), put(merged_got, 1 - c, 3)]
    for copy in copies[2:]:
        copy.start()
    for copy in copies:
        copy.wait()


def hybrid(n_seq, chunk_heads, queries, new_keys, new_values, key_cache, value_cache, selection):
    n = 4
    rows, features = queries.shape
    width = features // n
    heads = width // HD
    chunks, first = [], 0
    for count in chunk_heads(heads):
        chunks.append((first * HD, count * HD))
        first += count
    factor = float(HD) ** (-0.5) * LOG2E
    blk_dev = key_cache.shape[0] // BLOCK
    picks = pltpu.with_memory_space_constraint(selection.T, pltpu.HBM)
    anywhere = pl.BlockSpec(memory_space=pl.ANY)
    in_hbm = pl.BlockSpec(memory_space=pltpu.HBM)
    resident = pl.BlockSpec(memory_space=pltpu.VMEM)
    bf16, f32 = jnp.bfloat16, jnp.float32

    def call(kernel, arrays, in_specs, shapes, scratch=(), scalars=(), result=None):
        return pl.pallas_call(
            kernel,
            out_shape=[pltpu.VMEM(*s) for s in shapes] if result is None else result,
            grid_spec=pltpu.PrefetchScalarGridSpec(
                num_scalar_prefetch=len(scalars),
                grid=(1,),
                in_specs=in_specs,
                out_specs=[resident] * len(shapes) if result is None else anywhere,
                scratch_shapes=list(scratch),
            ),
            input_output_aliases={6: 0} if len(arrays) == 7 and result is not None else {},
            compiler_params=pltpu.CompilerParams(vmem_limit_bytes=VMEM_LIMIT),
        )(*scalars, *arrays)

    def move(x, pairs, axes=("head", "sub")):
        return lax.ppermute(x, axes, list(pairs))

    def apart(d, sources=range(n)):
        return [(i, i ^ d) for i in sources]

    arrays = [pltpu.with_memory_space_constraint(x, pltpu.HBM) for x in (queries, new_keys, new_values)]
    caches = [pltpu.with_memory_space_constraint(x, pltpu.HBM) for x in (key_cache, value_cache)]
    from_args = [in_hbm] * 3 + [anywhere]

    def cross(i, after):
        size = chunks[i][1]
        sent = call(
            functools.partial(cross_kernel, width, chunks[i], chunks if i == 0 else ()),
            arrays + [after], from_args, [((rows, 2 * size), bf16)] * 2,
            [pltpu.SemaphoreType.DMA((4,))],
        )
        sources = range(n) if i == 0 else (0, 1)
        return sent, [move(sent[d - 2], apart(d, sources)) for d in (2, 3)]

    def cores(i, flip, after):
        start, size = chunks[i]
        return call(
            functools.partial(core_kernel, width, start, size, flip),
            arrays + [after], from_args, [((rows, 6 * size), bf16)],
            [pltpu.SemaphoreType.DMA((6,))],
        )[0]

    sends = call(
        functools.partial(sends_kernel, n_seq, blk_dev, rows, chunks),
        caches, [in_hbm] * 2,
        [((2 * BLOCK, size), bf16) for _, size in chunks for _ in range(n_seq)]
        + [((2 * rows, pl.cdiv(2 * rows, HD) * HD), f32)],
        [pltpu.SemaphoreType.DMA((2 * n_seq * len(chunks),))], [picks],
    )
    bias = sends[-1]
    sent, crossing = [sends[1]], []
    for i in range(len(chunks)):
        sent, came = cross(i, sent[0])
        crossing.append(came)
    own, par, after = [], [], sent[0]
    for i in range(len(chunks)):
        after = cores(i, 1, after)
        par.append(move(after, apart(1)))
    for i in range(len(chunks)):
        after = cores(i, 0, after)
        own.append(after)

    def fetch(i):
        block = sends[n_seq * i : n_seq * (i + 1)]
        came = [block[0]]
        for d in range(1, n_seq):
            came.append(move(block[d], [(z, z ^ d) for z in range(n_seq)], "seq"))
        kept = call(
            functools.partial(collect_kernel, blk_dev), came, [resident] * n_seq,
            [((4 * BLOCK, chunks[i][1]), bf16)], (), [picks],
        )[0]
        return kept, move(kept, apart(2, (2, 3)))

    result = None
    for i, (start, size) in enumerate(chunks):
        kept, crossed = fetch(i)
        per = 2 if size // HD % 2 == 0 else 1
        both = [own[i], par[i]]
        held_f32, held_bf16 = ((rows, size + HD), f32), ((rows, size + HD), bf16)
        a0, a1, b0, b1 = call(
            functools.partial(span_kernel, per, size, factor), [bias] + both,
            [resident] * 3, [held_f32] * 4,
        )
        s0, s1 = call(
            functools.partial(other_kernel, per, size, start, factor),
            both + crossing[i] + crossing[0] + [b0, b1], [resident] * 8, [held_f32] * 2,
        )
        loc0, loc1, part0, part1 = call(
            functools.partial(early_kernel, per, size, start, factor),
            both + crossing[0] + [kept, a0, a1, s0, s1], [resident] * 9,
            [held_f32] * 2 + [held_bf16] * 2,
        )
        far0 = move(part0, apart(2, (0, 1)))
        far1 = move(part1, apart(3, (0, 1)))
        got_loc = move(loc1, apart(1))
        out0, out1 = call(
            functools.partial(late_kernel, per, size, factor),
            both + [kept, crossed, b0, b1, s0, s1], [resident] * 8, [((rows, size), bf16)] * 2,
        )
        got = move(out1, apart(1))
        pieces = [out0, got, loc0, got_loc, far0, far1]
        specs = [resident] * 6
        if result is not None:
            pieces, specs = pieces + [result], specs + [anywhere]
        result = call(
            functools.partial(finish_kernel, width, start, size, len(pieces)),
            pieces, specs, [],
            [pltpu.VMEM((rows, size), bf16)] * 2 + [pltpu.SemaphoreType.DMA((4,))],
            (), jax.ShapeDtypeStruct((rows, features), bf16),
        )
    return result


def uneven(heads):
    second = max(2, heads * 3 // 8 // 2 * 2)
    return (heads - second, second)


def placed_map(body, mesh, placed):
    return jax.shard_map(
        body,
        mesh=mesh,
        in_specs=placed,
        out_specs=P(("groups", "seq", "head", "sub"), None),
        check_vma=False,
    )


def solution(mesh):
    subs = mesh.shape["sub"]
    n = mesh.shape["head"] * subs
    placed = (
        P(("groups", "seq", "head", "sub"), None),
        P(("groups", "seq", "head", "sub"), None),
        P(("groups", "seq", "head", "sub"), None),
        P(("groups", "seq"), ("head", "sub")),
        P(("groups", "seq"), ("head", "sub")),
        P("groups", None),
    )
    n_seq = mesh.shape["seq"]
    body = functools.partial(ulysses, n, subs)
    if (mesh.shape["head"], subs, n_seq) == (2, 2, 4):
        body = functools.partial(hybrid, n_seq, uneven)
    if (mesh.shape["head"], subs, n_seq) != (2, 2, 4):
        return placed_map(body, mesh, placed)

    def step(*args):
        return body(*args)

    return placed_map(step, mesh, placed)
```

```python
import functools

import jax
import jax.numpy as jnp
from jax import lax
from jax.experimental import pallas as pl
from jax.experimental.pallas import tpu as pltpu
from jax.sharding import PartitionSpec as P


HD = 128
BLOCK = 64
LOG2E = 1.4426950408889634
MASKED = -1e30
VMEM_LIMIT = 16 << 20


def softmax_rows(scores, values):
    top = functools.reduce(jnp.maximum, [jnp.max(s, axis=1, keepdims=True) for s in scores])
    weights = [jnp.exp2(s - top) for s in scores]
    total = functools.reduce(jnp.add, [jnp.sum(w, axis=1, keepdims=True) for w in weights])
    mixed = functools.reduce(
        jnp.add,
        [
            jnp.dot(w.astype(jnp.bfloat16), v, preferred_element_type=jnp.float32)
            for w, v in zip(weights, values)
        ],
    )
    return mixed, top, total


def logits(q, k, factor):
    return lax.dot_general(
        q, k, (((1,), (1,)), ((), ())), preferred_element_type=jnp.float32
    ) * factor


def ulysses_kernel(n, topk, per, parts, factor, where_ref, own_ref, *refs):
    qs, ks, vs = refs[:n], refs[n : 2 * n], refs[2 * n : 3 * n]
    cks, cvs = refs[3 * n : 3 * n + topk], refs[3 * n + topk : 3 * n + 2 * topk]
    out_ref, q_all, k_all, v_all = refs[3 * n + 2 * topk :]
    rows = qs[0].shape[0]
    count = rows * n
    for b in range(n):
        at = pl.ds(pl.multiple_of(where_ref[1 + b] * rows, rows), rows)
        q_all[at, :] = qs[b][...]
        k_all[at, :] = ks[b][...]
        v_all[at, :] = vs[b][...]
    step = count // parts
    causal = lax.broadcasted_iota(jnp.int32, (step, step), 0) >= lax.broadcasted_iota(
        jnp.int32, (step, step), 1
    )
    for j in range(per):
        col = slice(j * HD, (j + 1) * HD)
        ck = [r[0, :, col] for r in cks]
        cv = [r[0, :, col] for r in cvs]
        ck = jnp.concatenate(ck, axis=0)
        cv = jnp.concatenate(cv, axis=0)
        for i in range(parts):
            here = slice(i * step, (i + 1) * step)
            q = q_all[here, col]
            scores = [logits(q, ck, factor)]
            values = [cv]
            if i > 0:
                scores.append(logits(q, k_all[: i * step, col], factor))
                values.append(v_all[: i * step, col])
            scores.append(jnp.where(causal, logits(q, k_all[here, col], factor), MASKED))
            values.append(v_all[here, col])
            mixed, _, total = softmax_rows(scores, values)
            out_ref[here, col] = (mixed / total).astype(jnp.bfloat16)


def ulysses(n, subs, queries, new_keys, new_values, key_cache, value_cache, selection):
    rows, features = queries.shape
    width = features // n
    heads = width // HD
    topk = selection.shape[1]
    me = lax.axis_index("seq")
    group = lax.axis_index("head") * subs + lax.axis_index("sub")

    def peer(b):
        return lax.rem(group + b, n)

    def exchange(b, piece):
        return lax.ppermute(piece, ("head", "sub"), [(i, (i + b) % n) for i in range(n)])

    def spread(array):
        pieces = [array]
        for b in range(1, n):
            piece = lax.dynamic_slice_in_dim(array, peer(b) * width, width, axis=1)
            pieces.append(exchange(b, piece))
        return pieces

    blk_dev = key_cache.shape[0] // BLOCK
    owner_of = selection // blk_dev
    inner = jnp.sum(jnp.where(owner_of == me, selection % blk_dev, 0), axis=1)
    mine = lax.dynamic_index_in_dim(selection, me, 0, keepdims=False) // blk_dev
    got = [
        lax.all_to_all(
            cache.reshape(blk_dev, BLOCK, -1)[inner], "seq", split_axis=0, concat_axis=0, tiled=True
        )
        for cache in (key_cache, value_cache)
    ]
    q_pieces, k_pieces, v_pieces = spread(queries), spread(new_keys), spread(new_values)
    from_of = jnp.stack([group] + [lax.rem(group + b, n) for b in range(n, 0, -1)]).astype(jnp.int32)
    per = 2 if heads % 2 == 0 else 1
    cols = per * HD
    own = pl.BlockSpec((rows, cols), lambda h, w, o: (0, w[0] * (heads // per) + h))
    other = pl.BlockSpec((rows, cols), lambda h, w, o: (0, h))
    cached = [
        pl.BlockSpec((1, BLOCK, cols), functools.partial(lambda t, h, w, o: (o[t], 0, h), t))
        for t in range(topk)
    ]
    count = rows * n
    out = pl.pallas_call(
        functools.partial(
            ulysses_kernel, n, topk, per, 2, float(HD) ** (-0.5) * LOG2E
        ),
        out_shape=jax.ShapeDtypeStruct((count, width), jnp.bfloat16),
        grid_spec=pltpu.PrefetchScalarGridSpec(
            num_scalar_prefetch=2,
            grid=(heads // per,),
            in_specs=([own] + [other] * (n - 1)) * 3 + cached * 2,
            out_specs=pl.BlockSpec((count, cols), lambda h, w, o: (0, h)),
            scratch_shapes=[pltpu.VMEM((count, cols), jnp.bfloat16)] * 3,
        ),
        name="attend",
    )(from_of, mine, *q_pieces, *k_pieces, *v_pieces, *([got[0]] * topk), *([got[1]] * topk))
    result = jnp.zeros((rows, features), jnp.bfloat16)
    for b in range(n):
        piece = lax.dynamic_slice_in_dim(out, peer(b) * rows, rows, axis=0)
        if b > 0:
            piece = exchange(b, piece)
        result = lax.dynamic_update_slice_in_dim(
            result, piece, lax.rem(group + n - b, n) * width, axis=1
        )
    return result


def chip_bias(bias, place, rows):
    def token(at):
        return jnp.where(at < rows, place * rows + at, (1 - place) * rows + at - rows)

    q = token(lax.broadcasted_iota(jnp.int32, bias.shape, 0))
    k = lax.broadcasted_iota(jnp.int32, bias.shape, 1)
    bias[...] = jnp.where((k >= 2 * rows) | (q >= token(k)), 0.0, MASKED)


def biased(scores, seen, bias):
    masked = min(bias.shape[1], scores.shape[1] - seen)
    parts = [scores[:, seen : seen + masked] + bias[:, :masked]]
    if seen > 0:
        parts.insert(0, scores[:, :seen])
    if scores.shape[1] > seen + masked:
        parts.append(scores[:, seen + masked :])
    return jnp.concatenate(parts, axis=1)


def soft(scores, values):
    top = jnp.max(scores, axis=1, keepdims=True)
    weights = jnp.exp2(scores - top)
    total = jnp.sum(weights, axis=1, keepdims=True)
    mixed = jnp.dot(weights.astype(jnp.bfloat16), values, preferred_element_type=jnp.float32)
    return mixed, top, total


def held(sel_ref, row, owner, blk_dev):
    inner = jnp.int32(0)
    for t in range(sel_ref.shape[0]):
        picked = sel_ref[t, row]
        match = lax.div(picked, jnp.int32(blk_dev)) == owner
        inner = jnp.where(match, lax.rem(picked, jnp.int32(blk_dev)), inner)
    return inner


def group_index():
    return lax.axis_index("head") * 2 + lax.axis_index("sub")


def run_copies(pairs, sems):
    copies = [pltpu.make_async_copy(a, b, sems.at[i]) for i, (a, b) in enumerate(pairs)]
    for copy in copies:
        copy.start()
    for copy in copies:
        copy.wait()


def cross_kernel(width, chunk, asked, q, k, v, after, two, three, sems):
    def pairs(wanted):
        result = []
        for out, d in ((two, 2), (three, 3)):
            to = 0
            for array, (start, size) in wanted:
                at = (group_index() ^ d) * width + start
                cols = pl.ds(pl.multiple_of(at, HD), size)
                result.append((array.at[:, cols], out.at[:, to : to + size]))
                to += size
        return result

    @pl.when(lax.axis_index("head") == 0)
    def _():
        run_copies(pairs([(k, chunk), (v, chunk)]), sems)

    @pl.when(lax.axis_index("head") == 1)
    def _():
        run_copies(pairs([(q, other) for other in asked]), sems)


def core_kernel(width, start, size, flip, q, k, v, after, out, sems):
    pairs = []
    for i in range(2):
        at = (2 * i + (lax.axis_index("sub") ^ flip)) * width + start
        cols = pl.ds(pl.multiple_of(at, HD), size)
        for t, array in enumerate((q, k, v)):
            to = (3 * i + t) * size
            pairs.append((array.at[:, cols], out.at[:, to : to + size]))
    run_copies(pairs, sems)


def sends_kernel(n_seq, blk_dev, rows, chunks, sel_ref, kc, vc, *refs):
    outs, bias, sems = refs[:-2], refs[-2], refs[-1]
    me = lax.axis_index("seq")
    pairs = []
    for i, (start, size) in enumerate(chunks):
        for d in range(n_seq):
            inner = held(sel_ref, me ^ d, me, blk_dev)
            at = pl.ds(pl.multiple_of(inner * BLOCK, BLOCK), BLOCK)
            to = outs[i * n_seq + d]
            pairs.append((kc.at[at, start : start + size], to.at[:BLOCK]))
            pairs.append((vc.at[at, start : start + size], to.at[BLOCK:]))
    copies = [pltpu.make_async_copy(a, b, sems.at[i]) for i, (a, b) in enumerate(pairs)]
    for copy in copies:
        copy.start()
    chip_bias(bias, lax.axis_index("sub"), rows)
    for copy in copies:
        copy.wait()


def collect_kernel(blk_dev, sel_ref, *refs):
    sources, kept = refs[:-1], refs[-1]
    me = lax.axis_index("seq")
    topk = sel_ref.shape[0]
    for t in range(topk):
        distance = lax.div(sel_ref[t, me], jnp.int32(blk_dev)) ^ me
        for d, source in enumerate(sources):

            @pl.when(distance == d)
            def _():
                kept[t * BLOCK : (t + 1) * BLOCK] = source[:BLOCK]
                kept[(topk + t) * BLOCK : (topk + t + 1) * BLOCK] = source[BLOCK:]


def lane_put(into, lane, column):
    lanes = lax.broadcasted_iota(jnp.int32, into.shape, 1)
    return jnp.where(lanes == lane, column, into)


def spread(x, width):
    whole, rest = divmod(width, x.shape[1])
    return jnp.concatenate([x] * whole + ([x[:, :rest]] if rest else []), axis=1)


def resume(scores, values, mixed, top, total):
    here = jnp.maximum(jnp.max(scores, axis=1, keepdims=True), top)
    weights = jnp.exp2(scores - spread(here, scores.shape[1]))
    carry = jnp.exp2(top - here)
    total = jnp.sum(weights, axis=1, keepdims=True) + total * carry
    more = jnp.dot(weights.astype(jnp.bfloat16), values, preferred_element_type=jnp.float32)
    return more + mixed * carry, here, total


class Rows:
    def __init__(self, size, first, second, wide=None):
        self.size, self.refs, self.rows, self.wide = size, (first, second), first.shape[0], wide

    def clear(self):
        for ref in self.refs:
            ref[:, self.size :] = jnp.zeros((self.rows, HD), jnp.float32)

    def put(self, col, mixed):
        for i, ref in enumerate(self.refs):
            ref[:, col] = mixed[i * self.rows : (i + 1) * self.rows].astype(ref.dtype)

    def put_lanes(self, stats):
        for i, ref in enumerate(self.refs):
            at = slice(i * self.rows, (i + 1) * self.rows)
            lanes = ref[:, self.size :]
            for head, top, total in stats:
                lanes = lane_put(lane_put(lanes, 2 * head, top[at]), 2 * head + 1, total[at])
            ref[:, self.size :] = lanes

    def put_wide(self, head, top, total):
        shape = (2 * self.rows, HD)
        self.wide[2 * head] = jnp.broadcast_to(top, shape)
        self.wide[2 * head + 1] = jnp.broadcast_to(total, shape)

    def get(self, col, head):
        mixed = jnp.concatenate([ref[:, col] for ref in self.refs], axis=0)
        return mixed, self.wide[2 * head], self.wide[2 * head + 1]


def each_head(per, size, work, after=None):
    def step(h, carry):
        stats = []
        for j in range(per):
            head = h * per + j
            stats.append(work(head, pl.ds(pl.multiple_of(head * HD, HD), HD)))
        if after is not None:
            after(stats)
        return carry

    lax.fori_loop(0, size // HD // per, step, 0)


def part_of(refs, size, t, head):
    at = pl.ds(pl.multiple_of(t * size + head * HD, HD), HD)
    return [ref[:, at] for ref in refs]


def rows_of(refs, size, t, head):
    return jnp.concatenate(part_of(refs, size, t, head), axis=0)


def span_kernel(per, size, factor, bias, own, par, a0, a1, aw, b0, b1, bw):
    def work(head, col):
        for base, rows in ((0, first), (3, second)):
            k, v = (rows_of((own, par), size, base + t, head) for t in (1, 2))
            scores = logits(rows_of((own, par), size, base, head), k, factor)
            mixed, top, total = soft(biased(scores, 0, bias), v)
            rows.put(col, mixed)
            rows.put_wide(head, top, total)
            if base == 0:
                stat = (head, top, total)
        return stat

    first, second = Rows(size, a0, a1, aw), Rows(size, b0, b1, bw)
    first.clear()
    each_head(per, size, work, first.put_lanes)


def other_kernel(per, size, asked_at, factor, own, par, two, three, q_two, q_three, b0, b1, bw, s0, s1, sw):
    second, result = Rows(size, b0, b1, bw), Rows(size, s0, s1, sw)

    def keep(head, col, mixed, top, total):
        result.put(col, mixed)
        result.put_wide(head, top, total)

    def on_first(head, col):
        k, v = (rows_of((own, par), size, t, head) for t in (1, 2))
        q = rows_of((q_two, q_three), asked_at, 1, head)
        keep(head, col, *soft(logits(q, k, factor), v))

    def on_second(head, col):
        k, v = (rows_of((two, three), size, t, head) for t in (0, 1))
        scores = logits(rows_of((own, par), size, 3, head), k, factor)
        keep(head, col, *resume(scores, v, *second.get(col, head)))

    @pl.when(lax.axis_index("head") == 0)
    def _():
        each_head(per, size, on_first)

    @pl.when(lax.axis_index("head") == 1)
    def _():
        each_head(per, size, on_second)


def early_kernel(
    per, size, asked_at, factor, own, par, q_two, q_three, kept, a0, a1, aw, s0, s1, sw, loc0, loc1, part0, part1
):
    heads = size // HD
    first, partial = Rows(size, a0, a1, aw), Rows(size, s0, s1, sw)
    loc, part = Rows(size, loc0, loc1), Rows(size, part0, part1)

    def on_first(head, col):
        k, v = kept[: 2 * BLOCK, col], kept[2 * BLOCK :, col]
        scores = logits(rows_of((own, par), size, 0, head), k, factor)
        mixed, top, total = resume(scores, v, *first.get(col, head))
        loc.put(col, mixed * (1.0 / total))
        scores = logits(rows_of((q_two, q_three), asked_at, 1, head), k, factor)
        mixed, top, total = resume(scores, v, *partial.get(col, head))
        part.put(col, mixed * (1.0 / total))
        return head, top, total

    @pl.when(lax.axis_index("head") == 0)
    def _():
        loc.clear()
        each_head(per, size, on_first, loc.put_lanes)
        for source, into in zip(loc.refs, part.refs):
            left = source[:, size:]
            packed = jnp.zeros_like(left)
            for t in range(3):
                piece = left.astype(jnp.bfloat16).astype(jnp.float32)
                left = left - piece
                packed = packed + (pltpu.roll(piece, 2 * heads * t, 1) if t > 0 else piece)
            into[:, size:] = packed.astype(jnp.bfloat16)

    @pl.when(lax.axis_index("head") == 1)
    def _():
        for source, into in zip(first.refs, loc.refs):
            into[...] = source[...]


def late_kernel(per, size, factor, own, par, kept, crossed, b0, b1, bw, s0, s1, sw, out0, out1):
    out = Rows(size, out0, out1)

    def run(cache, second):
        def work(head, col):
            scores = logits(rows_of((own, par), size, 3, head), cache[: 2 * BLOCK, col], factor)
            mixed, _, total = resume(scores, cache[2 * BLOCK :, col], *second.get(col, head))
            out.put(col, mixed * (1.0 / total))

        each_head(per, size, work)

    @pl.when(lax.axis_index("head") == 0)
    def _():
        run(crossed, Rows(size, b0, b1, bw))

    @pl.when(lax.axis_index("head") == 1)
    def _():
        run(kept, Rows(size, s0, s1, sw))


def finish_kernel(width, start, size, count, *refs):
    own, got, loc_own, loc_got, far_own, far_got = refs[:6]
    result, merged_own, merged_got, sems = refs[count:]
    heads = size // HD
    c = lax.axis_index("sub")

    def put(array, group, i):
        to = pl.ds(pl.multiple_of(group * width + start, HD), size)
        return pltpu.make_async_copy(array, result.at[:, to], sems.at[i])

    copies = [put(own, 2 + c, 0), put(got, 3 - c, 1)]
    for copy in copies:
        copy.start()
    pairs = ((loc_own, far_own, merged_own), (loc_got, far_got, merged_got))

    @pl.when(lax.axis_index("head") == 0)
    def _():
        for loc, far, merged in pairs:
            merged[...] = loc[:, :size].astype(jnp.bfloat16)

    @pl.when(lax.axis_index("head") == 1)
    def _():
        for loc, far, merged in pairs:
            packed = far[:, size:].astype(jnp.float32)
            there = packed
            for t in range(1, 3):
                there = there + pltpu.roll(packed, HD - 2 * heads * t, 1)
            here = loc[:, size:]
            for i in range(heads):
                col = slice(i * HD, (i + 1) * HD)
                near_top, near_sum = here[:, 2 * i : 2 * i + 1], here[:, 2 * i + 1 : 2 * i + 2]
                far_top, far_sum = there[:, 2 * i : 2 * i + 1], there[:, 2 * i + 1 : 2 * i + 2]
                top = jnp.maximum(near_top, far_top)
                near = jnp.exp2(near_top - top)
                away = far_sum * jnp.exp2(far_top - top)
                scale = 1.0 / (near_sum * near + away)
                mixed = loc[:, col] * (near * scale)
                mixed = mixed + far[:, col].astype(jnp.float32) * (away * scale)
                merged[:, col] = mixed.astype(jnp.bfloat16)

    copies += [put(merged_own, c, 2), put(merged_got, 1 - c, 3)]
    for copy in copies[2:]:
        copy.start()
    for copy in copies:
        copy.wait()


def hybrid(n_seq, chunk_heads, queries, new_keys, new_values, key_cache, value_cache, selection):
    n = 4
    rows, features = queries.shape
    width = features // n
    heads = width // HD
    chunks, first = [], 0
    for count in chunk_heads(heads):
        chunks.append((first * HD, count * HD))
        first += count
    factor = float(HD) ** (-0.5) * LOG2E
    blk_dev = key_cache.shape[0] // BLOCK
    picks = pltpu.with_memory_space_constraint(selection.T, pltpu.HBM)
    anywhere = pl.BlockSpec(memory_space=pl.ANY)
    in_hbm = pl.BlockSpec(memory_space=pltpu.HBM)
    resident = pl.BlockSpec(memory_space=pltpu.VMEM)
    bf16, f32 = jnp.bfloat16, jnp.float32

    def call(kernel, arrays, in_specs, shapes, scratch=(), scalars=(), result=None):
        return pl.pallas_call(
            kernel,
            out_shape=[pltpu.VMEM(*s) for s in shapes] if result is None else result,
            grid_spec=pltpu.PrefetchScalarGridSpec(
                num_scalar_prefetch=len(scalars),
                grid=(1,),
                in_specs=in_specs,
                out_specs=[resident] * len(shapes) if result is None else anywhere,
                scratch_shapes=list(scratch),
            ),
            input_output_aliases={6: 0} if len(arrays) == 7 and result is not None else {},
            compiler_params=pltpu.CompilerParams(vmem_limit_bytes=VMEM_LIMIT),
        )(*scalars, *arrays)

    def move(x, pairs, axes=("head", "sub")):
        return lax.ppermute(x, axes, list(pairs))

    def apart(d, sources=range(n)):
        return [(i, i ^ d) for i in sources]

    arrays = [pltpu.with_memory_space_constraint(x, pltpu.HBM) for x in (queries, new_keys, new_values)]
    caches = [pltpu.with_memory_space_constraint(x, pltpu.HBM) for x in (key_cache, value_cache)]
    from_args = [in_hbm] * 3 + [anywhere]

    def cross(i, after):
        size = chunks[i][1]
        sent = call(
            functools.partial(cross_kernel, width, chunks[i], chunks if i == 0 else ()),
            arrays + [after], from_args, [((rows, 2 * size), bf16)] * 2,
            [pltpu.SemaphoreType.DMA((4,))],
        )
        sources = range(n) if i == 0 else (0, 1)
        return sent, [move(sent[d - 2], apart(d, sources)) for d in (2, 3)]

    def cores(i, flip, after):
        start, size = chunks[i]
        return call(
            functools.partial(core_kernel, width, start, size, flip),
            arrays + [after], from_args, [((rows, 6 * size), bf16)],
            [pltpu.SemaphoreType.DMA((6,))],
        )[0]

    sends = call(
        functools.partial(sends_kernel, n_seq, blk_dev, rows, chunks),
        caches, [in_hbm] * 2,
        [((2 * BLOCK, size), bf16) for _, size in chunks for _ in range(n_seq)]
        + [((2 * rows, pl.cdiv(2 * rows, HD) * HD), f32)],
        [pltpu.SemaphoreType.DMA((2 * n_seq * len(chunks),))], [picks],
    )
    bias = sends[-1]
    sent, crossing = [sends[1]], []
    for i in range(len(chunks)):
        sent, came = cross(i, sent[0])
        crossing.append(came)
    own, par, after = [], [], sent[0]
    for i in range(len(chunks)):
        after = cores(i, 1, after)
        par.append(move(after, apart(1)))
    for i in range(len(chunks)):
        after = cores(i, 0, after)
        own.append(after)

    def fetch(i):
        block = sends[n_seq * i : n_seq * (i + 1)]
        came = [block[0]]
        for d in range(1, n_seq):
            came.append(move(block[d], [(z, z ^ d) for z in range(n_seq)], "seq"))
        kept = call(
            functools.partial(collect_kernel, blk_dev), came, [resident] * n_seq,
            [((4 * BLOCK, chunks[i][1]), bf16)], (), [picks],
        )[0]
        return kept, move(kept, apart(2, (2, 3)))

    result = None
    for i, (start, size) in enumerate(chunks):
        kept, crossed = fetch(i)
        per = max(p for p in (5, 3, 2, 1) if size // HD % p == 0)
        both = [own[i], par[i]]
        held_f32, held_bf16 = ((rows, size + HD), f32), ((rows, size + HD), bf16)
        plain = ((rows, size), f32)
        wide = ((2 * size // HD, 2 * rows, HD), f32)
        a0, a1, aw, b0, b1, bw = call(
            functools.partial(span_kernel, per, size, factor), [bias] + both,
            [resident] * 3, [held_f32] * 2 + [wide] + [plain] * 2 + [wide],
        )
        s0, s1, sw = call(
            functools.partial(other_kernel, per, size, start, factor),
            both + crossing[i] + crossing[0] + [b0, b1, bw], [resident] * 9, [plain] * 2 + [wide],
        )
        loc0, loc1, part0, part1 = call(
            functools.partial(early_kernel, per, size, start, factor),
            both + crossing[0] + [kept, a0, a1, aw, s0, s1, sw], [resident] * 11,
            [held_f32] * 2 + [held_bf16] * 2,
        )
        far0 = move(part0, apart(2, (0, 1)))
        far1 = move(part1, apart(3, (0, 1)))
        got_loc = move(loc1, apart(1))
        out0, out1 = call(
            functools.partial(late_kernel, per, size, factor),
            both + [kept, crossed, b0, b1, bw, s0, s1, sw], [resident] * 10, [((rows, size), bf16)] * 2,
        )
        got = move(out1, apart(1))
        pieces = [out0, got, loc0, got_loc, far0, far1]
        specs = [resident] * 6
        if result is not None:
            pieces, specs = pieces + [result], specs + [anywhere]
        result = call(
            functools.partial(finish_kernel, width, start, size, len(pieces)),
            pieces, specs, [],
            [pltpu.VMEM((rows, size), bf16)] * 2 + [pltpu.SemaphoreType.DMA((4,))],
            (), jax.ShapeDtypeStruct((rows, features), bf16),
        )
    return result


def uneven(heads):
    second = max(2, heads * 3 // 8 // 2 * 2)
    return (heads - second, second)


def placed_map(body, mesh, placed):
    return jax.shard_map(
        body,
        mesh=mesh,
        in_specs=placed,
        out_specs=P(("groups", "seq", "head", "sub"), None),
        check_vma=False,
    )


def solution(mesh):
    subs = mesh.shape["sub"]
    n = mesh.shape["head"] * subs
    placed = (
        P(("groups", "seq", "head", "sub"), None),
        P(("groups", "seq", "head", "sub"), None),
        P(("groups", "seq", "head", "sub"), None),
        P(("groups", "seq"), ("head", "sub")),
        P(("groups", "seq"), ("head", "sub")),
        P("groups", None),
    )
    n_seq = mesh.shape["seq"]
    body = functools.partial(ulysses, n, subs)
    if (mesh.shape["head"], subs, n_seq) == (2, 2, 4):
        body = functools.partial(hybrid, n_seq, uneven)
    if (mesh.shape["head"], subs, n_seq) != (2, 2, 4):
        return placed_map(body, mesh, placed)

    def step(*args):
        return body(*args)

    return placed_map(step, mesh, placed)
```

```python
import functools

import jax
import jax.numpy as jnp
from jax import lax
from jax.experimental import pallas as pl
from jax.experimental.pallas import tpu as pltpu
from jax.sharding import PartitionSpec as P


HD = 128
BLOCK = 64
LOG2E = 1.4426950408889634
MASKED = -1e30
VMEM_LIMIT = 16 << 20


def softmax_rows(scores, values):
    top = functools.reduce(jnp.maximum, [jnp.max(s, axis=1, keepdims=True) for s in scores])
    weights = [jnp.exp2(s - top) for s in scores]
    total = functools.reduce(jnp.add, [jnp.sum(w, axis=1, keepdims=True) for w in weights])
    mixed = functools.reduce(
        jnp.add,
        [
            jnp.dot(w.astype(jnp.bfloat16), v, preferred_element_type=jnp.float32)
            for w, v in zip(weights, values)
        ],
    )
    return mixed, top, total


def logits(q, k, factor):
    return lax.dot_general(
        q, k, (((1,), (1,)), ((), ())), preferred_element_type=jnp.float32
    ) * factor


def ulysses_kernel(n, topk, per, parts, factor, where_ref, own_ref, *refs):
    qs, ks, vs = refs[:n], refs[n : 2 * n], refs[2 * n : 3 * n]
    cks, cvs = refs[3 * n : 3 * n + topk], refs[3 * n + topk : 3 * n + 2 * topk]
    out_ref, q_all, k_all, v_all = refs[3 * n + 2 * topk :]
    rows = qs[0].shape[0]
    count = rows * n
    for b in range(n):
        at = pl.ds(pl.multiple_of(where_ref[1 + b] * rows, rows), rows)
        q_all[at, :] = qs[b][...]
        k_all[at, :] = ks[b][...]
        v_all[at, :] = vs[b][...]
    step = count // parts
    causal = lax.broadcasted_iota(jnp.int32, (step, step), 0) >= lax.broadcasted_iota(
        jnp.int32, (step, step), 1
    )
    for j in range(per):
        col = slice(j * HD, (j + 1) * HD)
        ck = [r[0, :, col] for r in cks]
        cv = [r[0, :, col] for r in cvs]
        ck = jnp.concatenate(ck, axis=0)
        cv = jnp.concatenate(cv, axis=0)
        for i in range(parts):
            here = slice(i * step, (i + 1) * step)
            q = q_all[here, col]
            scores = [logits(q, ck, factor)]
            values = [cv]
            if i > 0:
                scores.append(logits(q, k_all[: i * step, col], factor))
                values.append(v_all[: i * step, col])
            scores.append(jnp.where(causal, logits(q, k_all[here, col], factor), MASKED))
            values.append(v_all[here, col])
            mixed, _, total = softmax_rows(scores, values)
            out_ref[here, col] = (mixed / total).astype(jnp.bfloat16)


def ulysses(n, subs, queries, new_keys, new_values, key_cache, value_cache, selection):
    rows, features = queries.shape
    width = features // n
    heads = width // HD
    topk = selection.shape[1]
    me = lax.axis_index("seq")
    group = lax.axis_index("head") * subs + lax.axis_index("sub")

    def peer(b):
        return lax.rem(group + b, n)

    def exchange(b, piece):
        return lax.ppermute(piece, ("head", "sub"), [(i, (i + b) % n) for i in range(n)])

    def spread(array):
        pieces = [array]
        for b in range(1, n):
            piece = lax.dynamic_slice_in_dim(array, peer(b) * width, width, axis=1)
            pieces.append(exchange(b, piece))
        return pieces

    blk_dev = key_cache.shape[0] // BLOCK
    owner_of = selection // blk_dev
    inner = jnp.sum(jnp.where(owner_of == me, selection % blk_dev, 0), axis=1)
    mine = lax.dynamic_index_in_dim(selection, me, 0, keepdims=False) // blk_dev
    got = [
        lax.all_to_all(
            cache.reshape(blk_dev, BLOCK, -1)[inner], "seq", split_axis=0, concat_axis=0, tiled=True
        )
        for cache in (key_cache, value_cache)
    ]
    q_pieces, k_pieces, v_pieces = spread(queries), spread(new_keys), spread(new_values)
    from_of = jnp.stack([group] + [lax.rem(group + b, n) for b in range(n, 0, -1)]).astype(jnp.int32)
    per = 2 if heads % 2 == 0 else 1
    cols = per * HD
    own = pl.BlockSpec((rows, cols), lambda h, w, o: (0, w[0] * (heads // per) + h))
    other = pl.BlockSpec((rows, cols), lambda h, w, o: (0, h))
    cached = [
        pl.BlockSpec((1, BLOCK, cols), functools.partial(lambda t, h, w, o: (o[t], 0, h), t))
        for t in range(topk)
    ]
    count = rows * n
    out = pl.pallas_call(
        functools.partial(
            ulysses_kernel, n, topk, per, 2, float(HD) ** (-0.5) * LOG2E
        ),
        out_shape=jax.ShapeDtypeStruct((count, width), jnp.bfloat16),
        grid_spec=pltpu.PrefetchScalarGridSpec(
            num_scalar_prefetch=2,
            grid=(heads // per,),
            in_specs=([own] + [other] * (n - 1)) * 3 + cached * 2,
            out_specs=pl.BlockSpec((count, cols), lambda h, w, o: (0, h)),
            scratch_shapes=[pltpu.VMEM((count, cols), jnp.bfloat16)] * 3,
        ),
        name="attend",
    )(from_of, mine, *q_pieces, *k_pieces, *v_pieces, *([got[0]] * topk), *([got[1]] * topk))
    result = jnp.zeros((rows, features), jnp.bfloat16)
    for b in range(n):
        piece = lax.dynamic_slice_in_dim(out, peer(b) * rows, rows, axis=0)
        if b > 0:
            piece = exchange(b, piece)
        result = lax.dynamic_update_slice_in_dim(
            result, piece, lax.rem(group + n - b, n) * width, axis=1
        )
    return result


def chip_bias(bias, place, rows):
    def token(at):
        return jnp.where(at < rows, place * rows + at, (1 - place) * rows + at - rows)

    q = token(lax.broadcasted_iota(jnp.int32, bias.shape, 0))
    k = lax.broadcasted_iota(jnp.int32, bias.shape, 1)
    bias[...] = jnp.where((k >= 2 * rows) | (q >= token(k)), 0.0, MASKED)


def biased(scores, seen, bias):
    masked = min(bias.shape[1], scores.shape[1] - seen)
    parts = [scores[:, seen : seen + masked] + bias[:, :masked]]
    if seen > 0:
        parts.insert(0, scores[:, :seen])
    if scores.shape[1] > seen + masked:
        parts.append(scores[:, seen + masked :])
    return jnp.concatenate(parts, axis=1)


def soft(scores, values):
    top = jnp.max(scores, axis=1, keepdims=True)
    weights = jnp.exp2(scores - top)
    total = jnp.sum(weights, axis=1, keepdims=True)
    mixed = jnp.dot(weights.astype(jnp.bfloat16), values, preferred_element_type=jnp.float32)
    return mixed, top, total


def held(sel_ref, row, owner, blk_dev):
    inner = jnp.int32(0)
    for t in range(sel_ref.shape[0]):
        picked = sel_ref[t, row]
        match = lax.div(picked, jnp.int32(blk_dev)) == owner
        inner = jnp.where(match, lax.rem(picked, jnp.int32(blk_dev)), inner)
    return inner


def group_index():
    return lax.axis_index("head") * 2 + lax.axis_index("sub")


def run_copies(pairs, sems):
    copies = [pltpu.make_async_copy(a, b, sems.at[i]) for i, (a, b) in enumerate(pairs)]
    for copy in copies:
        copy.start()
    for copy in copies:
        copy.wait()


def cross_kernel(width, chunk, asked, q, k, v, after, two, three, sems):
    def pairs(wanted):
        result = []
        for out, d in ((two, 2), (three, 3)):
            to = 0
            for array, (start, size) in wanted:
                at = (group_index() ^ d) * width + start
                cols = pl.ds(pl.multiple_of(at, HD), size)
                result.append((array.at[:, cols], out.at[:, to : to + size]))
                to += size
        return result

    @pl.when(lax.axis_index("head") == 0)
    def _():
        run_copies(pairs([(k, chunk), (v, chunk)]), sems)

    @pl.when(lax.axis_index("head") == 1)
    def _():
        run_copies(pairs([(q, other) for other in asked]), sems)


def core_kernel(width, start, size, flip, q, k, v, after, out, sems):
    pairs = []
    for i in range(2):
        at = (2 * i + (lax.axis_index("sub") ^ flip)) * width + start
        cols = pl.ds(pl.multiple_of(at, HD), size)
        for t, array in enumerate((q, k, v)):
            to = (3 * i + t) * size
            pairs.append((array.at[:, cols], out.at[:, to : to + size]))
    run_copies(pairs, sems)


def sends_kernel(blk_dev, rows, wanted, sel_ref, kc, vc, *refs):
    outs, rest = refs[: len(wanted)], refs[len(wanted) :]
    me = lax.axis_index("seq")
    pairs = []
    for out, (d, (start, size)) in zip(outs, wanted):
        inner = held(sel_ref, me ^ d, me, blk_dev)
        at = pl.ds(pl.multiple_of(inner * BLOCK, BLOCK), BLOCK)
        pairs.append((kc.at[at, start : start + size], out.at[:BLOCK]))
        pairs.append((vc.at[at, start : start + size], out.at[BLOCK:]))
    copies = [pltpu.make_async_copy(a, b, rest[-1].at[i]) for i, (a, b) in enumerate(pairs)]
    for copy in copies:
        copy.start()
    for bias in rest[:-1]:
        chip_bias(bias, lax.axis_index("sub"), rows)
    for copy in copies:
        copy.wait()


def collect_kernel(blk_dev, sel_ref, *refs):
    sources, kept = refs[:-1], refs[-1]
    me = lax.axis_index("seq")
    topk = sel_ref.shape[0]
    for t in range(topk):
        distance = lax.div(sel_ref[t, me], jnp.int32(blk_dev)) ^ me
        for d, source in enumerate(sources):

            @pl.when(distance == d)
            def _():
                kept[t * BLOCK : (t + 1) * BLOCK] = source[:BLOCK]
                kept[(topk + t) * BLOCK : (topk + t + 1) * BLOCK] = source[BLOCK:]


def lane_put(into, lane, column):
    lanes = lax.broadcasted_iota(jnp.int32, into.shape, 1)
    return jnp.where(lanes == lane, column, into)


def spread(x, width):
    whole, rest = divmod(width, x.shape[1])
    return jnp.concatenate([x] * whole + ([x[:, :rest]] if rest else []), axis=1)


def resume(scores, values, mixed, top, total):
    here = jnp.maximum(jnp.max(scores, axis=1, keepdims=True), top)
    weights = jnp.exp2(scores - spread(here, scores.shape[1]))
    carry = jnp.exp2(top - here)
    total = jnp.sum(weights, axis=1, keepdims=True) + total * carry
    more = jnp.dot(weights.astype(jnp.bfloat16), values, preferred_element_type=jnp.float32)
    return more + mixed * carry, here, total


class Rows:
    def __init__(self, size, first, second, wide=None):
        self.size, self.refs, self.rows, self.wide = size, (first, second), first.shape[0], wide

    def clear(self):
        for ref in self.refs:
            ref[:, self.size :] = jnp.zeros((self.rows, HD), jnp.float32)

    def put(self, col, mixed):
        for i, ref in enumerate(self.refs):
            ref[:, col] = mixed[i * self.rows : (i + 1) * self.rows].astype(ref.dtype)

    def put_lanes(self, stats):
        for i, ref in enumerate(self.refs):
            at = slice(i * self.rows, (i + 1) * self.rows)
            lanes = ref[:, self.size :]
            for head, top, total in stats:
                lanes = lane_put(lane_put(lanes, 2 * head, top[at]), 2 * head + 1, total[at])
            ref[:, self.size :] = lanes

    def put_wide(self, head, top, total):
        shape = (2 * self.rows, HD)
        self.wide[2 * head] = jnp.broadcast_to(top, shape)
        self.wide[2 * head + 1] = jnp.broadcast_to(total, shape)

    def get(self, col, head):
        mixed = jnp.concatenate([ref[:, col] for ref in self.refs], axis=0)
        return mixed, self.wide[2 * head], self.wide[2 * head + 1]


def each_head(per, size, work, after=None):
    def step(h, carry):
        stats = []
        for j in range(per):
            head = h * per + j
            stats.append(work(head, pl.ds(pl.multiple_of(head * HD, HD), HD)))
        if after is not None:
            after(stats)
        return carry

    lax.fori_loop(0, size // HD // per, step, 0)


def part_of(refs, size, t, head):
    at = pl.ds(pl.multiple_of(t * size + head * HD, HD), HD)
    return [ref[:, at] for ref in refs]


def rows_of(refs, size, t, head):
    return jnp.concatenate(part_of(refs, size, t, head), axis=0)


def span_kernel(per, size, factor, bias, own, par, a0, a1, aw, b0, b1, bw):
    def work(head, col):
        for base, rows in ((0, first), (3, second)):
            k, v = (rows_of((own, par), size, base + t, head) for t in (1, 2))
            scores = logits(rows_of((own, par), size, base, head), k, factor)
            mixed, top, total = soft(biased(scores, 0, bias), v)
            rows.put(col, mixed)
            rows.put_wide(head, top, total)
            if base == 0:
                stat = (head, top, total)
        return stat

    first, second = Rows(size, a0, a1, aw), Rows(size, b0, b1, bw)
    first.clear()
    each_head(per, size, work, first.put_lanes)


def other_kernel(per, size, asked_at, factor, own, par, two, three, q_two, q_three, b0, b1, bw, s0, s1, sw):
    second, result = Rows(size, b0, b1, bw), Rows(size, s0, s1, sw)

    def keep(head, col, mixed, top, total):
        result.put(col, mixed)
        result.put_wide(head, top, total)

    def on_first(head, col):
        k, v = (rows_of((own, par), size, t, head) for t in (1, 2))
        q = rows_of((q_two, q_three), asked_at, 1, head)
        keep(head, col, *soft(logits(q, k, factor), v))

    def on_second(head, col):
        k, v = (rows_of((two, three), size, t, head) for t in (0, 1))
        scores = logits(rows_of((own, par), size, 3, head), k, factor)
        keep(head, col, *resume(scores, v, *second.get(col, head)))

    @pl.when(lax.axis_index("head") == 0)
    def _():
        each_head(per, size, on_first)

    @pl.when(lax.axis_index("head") == 1)
    def _():
        each_head(per, size, on_second)


def early_kernel(
    per, size, asked_at, factor, own, par, q_two, q_three, kept, a0, a1, aw, s0, s1, sw, *refs
):
    heads = size // HD
    first, partial = Rows(size, a0, a1, aw), Rows(size, s0, s1, sw)
    loc, part, stats = Rows(size, *refs[:2]), Rows(size, *refs[2:4]), Rows(0, *refs[4:])

    def on_first(head, col):
        k, v = kept[: 2 * BLOCK, col], kept[2 * BLOCK :, col]
        scores = logits(rows_of((own, par), size, 0, head), k, factor)
        mixed, top, total = resume(scores, v, *first.get(col, head))
        loc.put(col, mixed)
        near = (head, top, total)
        scores = logits(rows_of((q_two, q_three), asked_at, 1, head), k, factor)
        mixed, top, total = resume(scores, v, *partial.get(col, head))
        part.put(col, mixed)
        return near, (head, top, total)

    def after(results):
        loc.put_lanes([near for near, _ in results])
        stats.put_lanes([far for _, far in results])

    @pl.when(lax.axis_index("head") == 0)
    def _():
        loc.clear()
        stats.clear()
        each_head(per, size, on_first, after)
        for source, into in zip(stats.refs, part.refs):
            left = source[...]
            packed = jnp.zeros_like(left)
            for t in range(3):
                piece = left.astype(jnp.bfloat16).astype(jnp.float32)
                left = left - piece
                packed = packed + (pltpu.roll(piece, 2 * heads * t, 1) if t > 0 else piece)
            into[:, size:] = packed.astype(jnp.bfloat16)

    @pl.when(lax.axis_index("head") == 1)
    def _():
        for source, into in zip(first.refs, loc.refs):
            into[...] = source[...]


def late_kernel(per, size, factor, own, par, kept, crossed, b0, b1, bw, s0, s1, sw, out0, out1):
    out = Rows(size, out0, out1)

    def run(cache, second):
        def work(head, col):
            scores = logits(rows_of((own, par), size, 3, head), cache[: 2 * BLOCK, col], factor)
            mixed, _, total = resume(scores, cache[2 * BLOCK :, col], *second.get(col, head))
            out.put(col, mixed * (1.0 / total))

        each_head(per, size, work)

    @pl.when(lax.axis_index("head") == 0)
    def _():
        run(crossed, Rows(size, b0, b1, bw))

    @pl.when(lax.axis_index("head") == 1)
    def _():
        run(kept, Rows(size, s0, s1, sw))


def finish_kernel(width, start, size, count, *refs):
    own, got, loc_own, loc_got, far_own, far_got = refs[:6]
    result, merged_own, merged_got, sems = refs[count:]
    heads = size // HD
    c = lax.axis_index("sub")

    def put(array, group, i):
        to = pl.ds(pl.multiple_of(group * width + start, HD), size)
        return pltpu.make_async_copy(array, result.at[:, to], sems.at[i])

    copies = [put(own, 2 + c, 0), put(got, 3 - c, 1)]
    for copy in copies:
        copy.start()
    copies += [put(merged_own, c, 2), put(merged_got, 1 - c, 3)]
    pairs = (
        (loc_own, far_own, merged_own, copies[2]), (loc_got, far_got, merged_got, copies[3])
    )

    @pl.when(lax.axis_index("head") == 0)
    def _():
        for loc, far, merged, copy in pairs:
            scales = 1.0 / loc[:, size:]
            for i in range(heads):
                col = slice(i * HD, (i + 1) * HD)
                mixed = loc[:, col] * scales[:, 2 * i + 1 : 2 * i + 2]
                merged[:, col] = mixed.astype(jnp.bfloat16)
            copy.start()

    @pl.when(lax.axis_index("head") == 1)
    def _():
        for loc, far, merged, copy in pairs:
            packed = far[:, size:].astype(jnp.float32)
            there = packed
            for t in range(1, 3):
                there = there + pltpu.roll(packed, HD - 2 * heads * t, 1)
            here = loc[:, size:]
            near_sum, far_sum = pltpu.roll(here, HD - 1, 1), pltpu.roll(there, HD - 1, 1)
            top = jnp.maximum(here, there)
            near, away = jnp.exp2(here - top), jnp.exp2(there - top)
            scale = 1.0 / (near_sum * near + far_sum * away)
            near, away = near * scale, away * scale
            for i in range(heads):
                col = slice(i * HD, (i + 1) * HD)
                mixed = loc[:, col] * near[:, 2 * i : 2 * i + 1]
                mixed = mixed + far[:, col].astype(jnp.float32) * away[:, 2 * i : 2 * i + 1]
                merged[:, col] = mixed.astype(jnp.bfloat16)
            copy.start()

    for copy in copies:
        copy.wait()


def hybrid(n_seq, chunk_heads, queries, new_keys, new_values, key_cache, value_cache, selection):
    n = 4
    rows, features = queries.shape
    width = features // n
    heads = width // HD
    chunks, first = [], 0
    for count in chunk_heads(heads):
        chunks.append((first * HD, count * HD))
        first += count
    factor = float(HD) ** (-0.5) * LOG2E
    blk_dev = key_cache.shape[0] // BLOCK
    picks = pltpu.with_memory_space_constraint(selection.T, pltpu.HBM)
    anywhere = pl.BlockSpec(memory_space=pl.ANY)
    in_hbm = pl.BlockSpec(memory_space=pltpu.HBM)
    resident = pl.BlockSpec(memory_space=pltpu.VMEM)
    bf16, f32 = jnp.bfloat16, jnp.float32

    def call(kernel, arrays, in_specs, shapes, scratch=(), scalars=(), result=None):
        return pl.pallas_call(
            kernel,
            out_shape=[pltpu.VMEM(*s) for s in shapes] if result is None else result,
            grid_spec=pltpu.PrefetchScalarGridSpec(
                num_scalar_prefetch=len(scalars),
                grid=(1,),
                in_specs=in_specs,
                out_specs=[resident] * len(shapes) if result is None else anywhere,
                scratch_shapes=list(scratch),
            ),
            input_output_aliases={6: 0} if len(arrays) == 7 and result is not None else {},
            compiler_params=pltpu.CompilerParams(vmem_limit_bytes=VMEM_LIMIT),
        )(*scalars, *arrays)

    def move(x, pairs, axes=("head", "sub")):
        return lax.ppermute(x, axes, list(pairs))

    def apart(d, sources=range(n)):
        return [(i, i ^ d) for i in sources]

    arrays = [pltpu.with_memory_space_constraint(x, pltpu.HBM) for x in (queries, new_keys, new_values)]
    caches = [pltpu.with_memory_space_constraint(x, pltpu.HBM) for x in (key_cache, value_cache)]
    from_args = [in_hbm] * 3 + [anywhere]

    def cross(i, after):
        size = chunks[i][1]
        sent = call(
            functools.partial(cross_kernel, width, chunks[i], chunks if i == 0 else ()),
            arrays + [after], from_args, [((rows, 2 * size), bf16)] * 2,
            [pltpu.SemaphoreType.DMA((4,))],
        )
        sources = range(n) if i == 0 else (0, 1)
        return sent, [move(sent[d - 2], apart(d, sources)) for d in (2, 3)]

    def cores(i, flip, after):
        start, size = chunks[i]
        return call(
            functools.partial(core_kernel, width, start, size, flip),
            arrays + [after], from_args, [((rows, 6 * size), bf16)],
            [pltpu.SemaphoreType.DMA((6,))],
        )[0]

    def blocks(wanted, extra=()):
        return call(
            functools.partial(sends_kernel, blk_dev, rows, wanted),
            caches, [in_hbm] * 2,
            [((2 * BLOCK, chunk[1]), bf16) for _, chunk in wanted] + list(extra),
            [pltpu.SemaphoreType.DMA((2 * len(wanted),))], [picks],
        )

    urgent = [(d, chunks[0]) for d in range(2, n_seq)]
    others = [(d, chunk) for chunk in chunks for d in range(n_seq) if (d, chunk) not in urgent]
    first_out = blocks(urgent)
    mask = ((2 * rows, pl.cdiv(2 * rows, HD) * HD), f32)
    *other_out, bias = blocks(others, [mask])
    sends = dict(zip(urgent + others, [*first_out, *other_out]))
    sent, crossing = [first_out[0]], []
    for i in range(len(chunks)):
        sent, came = cross(i, sent[0])
        crossing.append(came)
    own, par, after = [], [], sent[0]
    for i in range(len(chunks)):
        after = cores(i, 1, after)
        par.append(move(after, apart(1)))
    for i in range(len(chunks)):
        after = cores(i, 0, after)
        own.append(after)

    def fetch(i):
        block = [sends[d, chunks[i]] for d in range(n_seq)]
        came = [block[0]]
        for d in range(1, n_seq):
            came.append(move(block[d], [(z, z ^ d) for z in range(n_seq)], "seq"))
        kept = call(
            functools.partial(collect_kernel, blk_dev), came, [resident] * n_seq,
            [((4 * BLOCK, chunks[i][1]), bf16)], (), [picks],
        )[0]
        return kept, move(kept, apart(2, (2, 3)))

    result = None
    for i, (start, size) in enumerate(chunks):
        kept, crossed = fetch(i)
        per = max(p for p in (5, 4, 3, 2, 1) if size // HD % p == 0)
        both = [own[i], par[i]]
        held_f32, held_bf16 = ((rows, size + HD), f32), ((rows, size + HD), bf16)
        plain = ((rows, size), f32)
        wide = ((2 * size // HD, 2 * rows, HD), f32)
        a0, a1, aw, b0, b1, bw = call(
            functools.partial(span_kernel, per, size, factor), [bias] + both,
            [resident] * 3, [held_f32] * 2 + [wide] + [plain] * 2 + [wide],
        )
        s0, s1, sw = call(
            functools.partial(other_kernel, per, size, start, factor),
            both + crossing[i] + crossing[0] + [b0, b1, bw], [resident] * 9, [plain] * 2 + [wide],
        )
        loc0, loc1, part0, part1 = call(
            functools.partial(early_kernel, per, size, start, factor),
            both + crossing[0] + [kept, a0, a1, aw, s0, s1, sw], [resident] * 11,
            [held_f32] * 2 + [held_bf16] * 2, [pltpu.VMEM((rows, HD), f32)] * 2,
        )
        far0 = move(part0, apart(2, (0, 1)))
        far1 = move(part1, apart(3, (0, 1)))
        got_loc = move(loc1, apart(1))
        out0, out1 = call(
            functools.partial(late_kernel, per, size, factor),
            both + [kept, crossed, b0, b1, bw, s0, s1, sw], [resident] * 10, [((rows, size), bf16)] * 2,
        )
        got = move(out1, apart(1))
        pieces = [out0, got, loc0, got_loc, far0, far1]
        specs = [resident] * 6
        if result is not None:
            pieces, specs = pieces + [result], specs + [anywhere]
        result = call(
            functools.partial(finish_kernel, width, start, size, len(pieces)),
            pieces, specs, [],
            [pltpu.VMEM((rows, size), bf16)] * 2 + [pltpu.SemaphoreType.DMA((4,))],
            (), jax.ShapeDtypeStruct((rows, features), bf16),
        )
    return result


def uneven(heads):
    second = max(2, heads * 3 // 8 // 2 * 2)
    return (heads - second, second)


def placed_map(body, mesh, placed):
    return jax.shard_map(
        body,
        mesh=mesh,
        in_specs=placed,
        out_specs=P(("groups", "seq", "head", "sub"), None),
        check_vma=False,
    )


def solution(mesh):
    subs = mesh.shape["sub"]
    n = mesh.shape["head"] * subs
    placed = (
        P(("groups", "seq", "head", "sub"), None),
        P(("groups", "seq", "head", "sub"), None),
        P(("groups", "seq", "head", "sub"), None),
        P(("groups", "seq"), ("head", "sub")),
        P(("groups", "seq"), ("head", "sub")),
        P("groups", None),
    )
    n_seq = mesh.shape["seq"]
    body = functools.partial(ulysses, n, subs)
    if (mesh.shape["head"], subs, n_seq) == (2, 2, 4):
        body = functools.partial(hybrid, n_seq, uneven)
    if (mesh.shape["head"], subs, n_seq) != (2, 2, 4):
        return placed_map(body, mesh, placed)

    def step(*args):
        return body(*args)

    return placed_map(step, mesh, placed)
```
